32 devices in a mesh: strike: 8 (over z, y), depth: 4 (over x, core).
Axes of the slice: x: 2, y: 2, z: 4, core: 2. Of those that a mesh axis runs over, the one named last changes fastest.
Arguments:
- velocity: float32 [3, 128, 64, 256], P(None, 'strike', 'depth'), may hold values from -6 to 6
- stress: float32 [6, 128, 64, 256], P(None, 'strike', 'depth'), may hold values from -6 to 6
- material: int32 [128, 64, 256], P('strike', 'depth'), may hold values from 0 to 3
- patch_order: int32 [48], replicated, may hold values from 0 to 47, each once
- fault_params: float32 [4, 64, 48], P(None, 'depth', 'strike'), may hold values from -5 to 5, as said below
Outputs:
- velocity_out: float32 [3, 128, 64, 256], P(None, 'strike', 'depth')
- slip_rate: float32 [64, 48], P('depth', 'strike')
The draws below stay inside these ranges and needn't reach their ends.
Inputs may be any that keep to these rules, and one draw needn't show every extreme that they name: `fault_params`: row 0 in 0.3 to 1.2, row 1 in -0.5 to 1.5, row 2 in 1 to 3, row 3 in -5 to 5. `patch_order`: each fault column exactly once.
All inputs are finite; a program needn't handle non-finite values.
Results may differ from the reference program's by a relative error of at most 0.0003.
Values sent between devices are 32-bit elements; how exact they have to be, the bound alone decides.
A program may use at most 64 MiB of HBM per device.

```python
import jax
import jax.numpy as jnp
from jax import lax

NY = 256
NEWTON = 8
NX = 128
NZ = 64
FAULT_ROW = 128
FAULT_START = 32
FAULT_COLS = 48


def draw_fault_params(key, part):
    keys = jax.random.split(jax.random.fold_in(key, 17), 4)
    shape = (NZ, FAULT_COLS)
    coef = jnp.exp(jax.random.uniform(keys[0], shape, jnp.float32, jnp.log(0.3), jnp.log(1.2)))
    psi = jax.random.uniform(keys[1], shape, jnp.float32, -0.5, 1.5)
    normal_stress = jax.random.uniform(keys[2], shape, jnp.float32, 1.0, 3.0)
    background = jnp.clip(1.5 * jax.random.normal(keys[3], shape, jnp.float32), -5.0, 5.0)
    return jnp.stack([coef, psi, normal_stress, background]).astype(jnp.float32)


def touch_ends(drawn, own_key, low, top_value):
    dims = drawn.shape
    index_at = [jax.random.randint(jax.random.fold_in(own_key, axis), (), 0, dims[axis]) for axis in range(len(dims))]
    drawn = drawn.at[tuple(index_at)].set(low)
    longest = dims.index(max(dims))
    index_at[longest] = (index_at[longest] + 1) % dims[longest]
    return drawn.at[tuple(index_at)].set(top_value)


def steps_of(rng, dims, cuts, least, top_value):
    gain = 1.0
    for dim, blocks in cuts:
        heights = jax.random.uniform(jax.random.fold_in(jax.random.fold_in(rng, 6), dim), (blocks,), jnp.float32, least / len(cuts), top_value / len(cuts))
        gain = gain * jnp.repeat(jnp.exp(heights), dims[dim] // blocks).reshape((-1,) + (1,) * (len(dims) - 1 - dim))
    return gain


def normal_values(own_key, extent, deviation, bound, cuts=(), held_as=jnp.bfloat16):
    gain = steps_of(own_key, extent, cuts, -0.22, 0.18) if cuts else 1.0
    array = jax.random.normal(own_key, extent, jnp.float32) * deviation * gain
    return jnp.minimum(jnp.maximum(array, -bound), bound).astype(held_as)


def setup_inputs(seed: int = 0) -> dict:
    key_list = jax.random.split(jax.random.key(seed), 6)
    return {
        "velocity": normal_values(key_list[0], (3, NX, NZ, NY), 1.0, 6.0, ((1, 8), (2, 4)), jnp.float32),
        "stress": normal_values(key_list[1], (6, NX, NZ, NY), 1.0, 6.0, ((1, 8), (2, 4)), jnp.float32),
        "material": touch_ends(jax.random.randint(key_list[2], (NX, NZ, NY), 0, 4), jax.random.fold_in(key_list[2], 1), 0, 3).astype(jnp.int32),
        "patch_order": jax.random.permutation(key_list[3], FAULT_COLS).astype(jnp.int32),
        "fault_params": draw_fault_params(jax.random.fold_in(key_list[5], 71), 0),
    }


BUOY = (1.0, 0.8, 0.6, 1.25)
C_ONE = 9.0 / 8.0
C_TWO = -1.0 / 24.0

def inverse_sinh(value):
    magnitude = jnp.log(jnp.abs(value) + jnp.sqrt(1.0 + value * value))
    return jnp.where(value < 0, -magnitude, magnitude)

def shifted(field, axis, width):
    pads = [(0, 0)] * field.ndim
    pads[axis] = (2, 2)
    padded = jnp.pad(field, pads)

    def part(offset):
        return lax.slice_in_dim(padded, 2 + offset, 2 + offset + width, axis=axis)
    return part

def minus_diff(field, axis):
    part = shifted(field, axis, field.shape[axis])
    return C_ONE * (part(0) - part(-1)) + C_TWO * (part(1) - part(-2))

def plus_diff(field, axis):
    part = shifted(field, axis, field.shape[axis])
    return C_ONE * (part(1) - part(0)) + C_TWO * (part(2) - part(-1))

def friction(tau_trial, params):
    coef, psi, normal_stress, background = (params[0], params[1], params[2], params[3])
    tau_total = tau_trial + background
    half_q = 0.5 * jnp.exp(psi / coef)
    scale = normal_stress * coef
    rate = jnp.zeros_like(tau_total)
    for step in range(NEWTON):
        arg_val = rate * half_q
        resid = tau_total - rate - scale * inverse_sinh(arg_val)
        slope = -1.0 - scale * half_q / jnp.sqrt(1.0 + arg_val * arg_val)
        rate = rate - 0.35 * resid / slope
    return rate

def reference(velocity, stress, material, patch_order, fault_params):
    buoyancy = jnp.zeros(material.shape, jnp.float32)
    for index in range(4):
        buoyancy = buoyancy + (material == index).astype(jnp.float32) * BUOY[index]
    dxx = minus_diff(stress[0], 0)
    vx = velocity[0] + 0.25 * buoyancy * (dxx + minus_diff(stress[3], 2) + minus_diff(stress[4], 1))
    vy = velocity[1] + 0.25 * buoyancy * (plus_diff(stress[3], 0) + plus_diff(stress[1], 2) + minus_diff(stress[5], 1))
    vz = velocity[2] + 0.25 * buoyancy * (plus_diff(stress[4], 0) + plus_diff(stress[5], 2) + plus_diff(stress[2], 1))
    cols = slice(FAULT_START, FAULT_START + FAULT_COLS)
    traction = (stress[3, cols, :, FAULT_ROW] + 0.5 * dxx[cols, :, FAULT_ROW]).T
    owned = traction[:, patch_order]
    slip_rate = friction(owned, fault_params)
    slip_cols = jnp.zeros_like(slip_rate).at[:, patch_order].set(slip_rate).T
    plus_side = vx[cols, :, FAULT_ROW]
    minus_side = vx[cols, :, FAULT_ROW - 1]
    middle = 0.5 * (plus_side + minus_side)
    vx = vx.at[cols, :, FAULT_ROW].set(middle + 0.5 * slip_cols)
    vx = vx.at[cols, :, FAULT_ROW - 1].set(middle - 0.5 * slip_cols)
    return (jnp.stack([vx, vy, vz]), slip_rate)
```

```python
import functools

import jax
import jax.numpy as jnp
from jax import lax
from jax.experimental import pallas as pl
from jax.experimental.pallas import tpu as pltpu
from jax.sharding import PartitionSpec as P

NEWTON = 8
BUOY = (1.0, 0.8, 0.6, 1.25)
C_ONE = 9.0 / 8.0
C_TWO = -1.0 / 24.0
MESH = pl.DeviceIdType.MESH


def inverse_sinh(value):
    magnitude = jnp.log(jnp.abs(value) + jnp.sqrt(1.0 + value * value))
    return jnp.where(value < 0, -magnitude, magnitude)


def friction(tau_total, coef, psi, normal_stress):
    half_q = 0.5 * jnp.exp(psi / coef)
    scale = normal_stress * coef
    rate = jnp.zeros_like(tau_total)
    for _ in range(NEWTON):
        arg_val = rate * half_q
        resid = tau_total - rate - scale * inverse_sinh(arg_val)
        slope = -1.0 - scale * half_q / jnp.sqrt(1.0 + arg_val * arg_val)
        rate = rate - 0.35 * resid / slope
    return rate


def kernel(
    dims, vel, st, mat, po, fp, out, slip,
    sx, so, vb, mb, pb, ownp, zlo, zhi, packs, recv,
    lsem, psend, precv, xsend, xrecv, zsend, zrecv,
):
    n, nd, cx, cz, ny, fc, wide = dims
    row = ny // 2
    per = fc // n
    first_tile = n // 4
    tiles = fc // cx
    me = lax.axis_index("strike")
    dep = lax.axis_index("depth")

    loads = [
        pltpu.make_async_copy(st.at[0], sx.at[0, pl.ds(2, cx)], lsem.at[0]),
        pltpu.make_async_copy(st.at[3], sx.at[1, pl.ds(2, cx)], lsem.at[1]),
        pltpu.make_async_copy(fp, pb, lsem.at[2]),
        pltpu.make_async_copy(st.at[4], sx.at[2, pl.ds(2, cx)], lsem.at[3]),
        pltpu.make_async_copy(st.at[2], so.at[1], lsem.at[4]),
        pltpu.make_async_copy(st.at[5], so.at[2], lsem.at[5]),
        pltpu.make_async_copy(st.at[1], so.at[0], lsem.at[6]),
        pltpu.make_async_copy(mat, mb, lsem.at[7]),
        pltpu.make_async_copy(vel, vb, lsem.at[8]),
    ]
    for load in loads:
        load.start()

    has_left, has_right = me > 0, me < n - 1
    has_below, has_above = dep > 0, dep < nd - 1
    barrier = pltpu.get_barrier_semaphore()
    for k in range(1, n):
        peer = lax.rem(me + k, n)
        pl.semaphore_signal(barrier, inc=1, device_id=(peer, dep), device_id_type=MESH)

    @pl.when(has_below)
    def _():
        pl.semaphore_signal(barrier, inc=1, device_id=(me, dep - 1), device_id_type=MESH)

    @pl.when(has_above)
    def _():
        pl.semaphore_signal(barrier, inc=1, device_id=(me, dep + 1), device_id_type=MESH)

    zero_row = jnp.zeros((2, cz, ny), jnp.float32)

    @pl.when(jnp.logical_not(has_left))
    def _():
        for f in range(3):
            sx[f, 0:2] = zero_row

    @pl.when(jnp.logical_not(has_right))
    def _():
        for f in range(3):
            sx[f, cx + 2 : cx + 4] = zero_row

    @pl.when(jnp.logical_not(has_below))
    def _():
        zlo[...] = jnp.zeros(zlo.shape, jnp.float32)

    @pl.when(jnp.logical_not(has_above))
    def _():
        zhi[...] = jnp.zeros(zhi.shape, jnp.float32)

    lane = lax.broadcasted_iota(jnp.int32, (cz, wide), 1)
    lane_one = lax.broadcasted_iota(jnp.int32, (cz, 128), 1)
    loads[0].wait()
    loads[1].wait()
    loads[2].wait()
    near = jnp.logical_and(me >= first_tile - 1, me <= first_tile + tiles)
    base = jnp.where(near, 4 * cx + (me - first_tile) * cx, -4 * wide)
    normal = jnp.zeros((cz, wide), jnp.float32)
    shear = jnp.zeros((cz, wide), jnp.float32)
    for i in range(cx):
        here = lane == base + i
        normal = jnp.where(here, sx[0, 2 + i, :, row : row + 1], normal)
        shear = jnp.where(here, sx[1, 2 + i, :, row : row + 1], shear)
    dxx = C_ONE * (normal - pltpu.roll(normal, 1, 1)) + C_TWO * (
        pltpu.roll(normal, wide - 1, 1) - pltpu.roll(normal, 2, 1)
    )
    share = shear + 0.5 * dxx
    share = jnp.where(jnp.logical_and(lane >= 4 * cx, lane < 4 * cx + fc), share, 0.0)
    blocks = [share for _ in range(tiles)]
    for f in range(4):
        mine = jnp.full((cz, 128), 1.0, jnp.float32)
        for j in range(per):
            column = po[me * per + j]
            value = pb[f, :, j : j + 1]
            mine = jnp.where(lane_one == cx + j, value, mine)
            for t in range(tiles):
                local = column - t * cx
                held = jnp.logical_and(local >= 0, local < cx)
                place = jnp.where(held, f * cx + local, -1)
                blocks[t] = jnp.where(lane == place, value, blocks[t])
        ownp[f] = mine
    for t in range(tiles):
        packs[t] = blocks[t]
    my_tile = jnp.clip(me - first_tile, 0, tiles - 1)
    recv[me] = packs[my_tile]

    for load in loads[3:6]:
        load.wait()
    pl.semaphore_wait(
        barrier, n - 1 + has_below.astype(jnp.int32) + has_above.astype(jnp.int32)
    )

    def pack_copy(k):
        peer = lax.rem(me + k, n)
        return pltpu.make_async_remote_copy(
            src_ref=packs.at[jnp.clip(peer - first_tile, 0, tiles - 1)],
            dst_ref=recv.at[me],
            send_sem=psend.at[k],
            recv_sem=precv.at[me],
            device_id=(peer, dep),
            device_id_type=MESH,
        )

    def pack_arrival(k):
        source = lax.rem(me + k, n)
        return pltpu.make_async_remote_copy(
            src_ref=packs.at[0],
            dst_ref=recv.at[source],
            send_sem=psend.at[k],
            recv_sem=precv.at[source],
            device_id=(source, dep),
            device_id_type=MESH,
        )

    def x_copy(f, up):
        if up:
            rows = 2 if f == 0 else 1
            src, dst, to = cx + 2 - rows, 2 - rows, me + 1
        else:
            rows = 1 if f == 0 else 2
            src, dst, to = 2, cx + 2, me - 1
        slot = f if up else 3 + f
        return pltpu.make_async_remote_copy(
            src_ref=sx.at[f, pl.ds(src, rows)],
            dst_ref=sx.at[f, pl.ds(dst, rows)],
            send_sem=xsend.at[slot],
            recv_sem=xrecv.at[slot],
            device_id=(to, dep),
            device_id_type=MESH,
        )

    def z_copy(f, up):
        field = (sx.at[2, pl.ds(2, cx)], so.at[2], so.at[1])[f]
        if up:
            rows = 1 if f == 2 else 2
            src, dst, to = cz - rows, zlo.at[f, :, pl.ds(8 - rows, rows)], dep + 1
        else:
            rows = 2 if f == 2 else 1
            src, dst, to = 0, zhi.at[f, :, pl.ds(0, rows)], dep - 1
        slot = f if up else 3 + f
        return pltpu.make_async_remote_copy(
            src_ref=field.at[:, pl.ds(src, rows)],
            dst_ref=dst,
            send_sem=zsend.at[slot],
            recv_sem=zrecv.at[slot],
            device_id=(me, to),
            device_id_type=MESH,
        )

    for k in range(1, n):
        pack_copy(k).start()

    @pl.when(has_above)
    def _():
        for f in range(3):
            z_copy(f, True).start()

    @pl.when(has_below)
    def _():
        for f in range(3):
            z_copy(f, False).start()

    @pl.when(has_right)
    def _():
        for f in range(3):
            x_copy(f, True).start()

    @pl.when(has_left)
    def _():
        for f in range(3):
            x_copy(f, False).start()

    for load in loads[6:]:
        load.wait()

    @pl.when(has_below)
    def _():
        for f in range(3):
            z_copy(f, True).wait_recv()

    @pl.when(has_above)
    def _():
        for f in range(3):
            z_copy(f, False).wait_recv()

    yi = lax.broadcasted_iota(jnp.int32, (cz, ny), 1)

    def y_at(field, offset):
        moved = pltpu.roll(field, (-offset) % ny, 1)
        keep = yi < ny - offset if offset > 0 else yi >= -offset
        return jnp.where(keep, moved, 0.0)

    def z_at(f, field, x):
        joined = jnp.concatenate([zlo[f, x], field, zhi[f, x]], axis=0)
        total = cz + 16
        return lambda offset: pltpu.roll(joined, (-offset) % total, 0)[8 : 8 + cz]

    def minus(at):
        return C_ONE * (at(0) - at(-1)) + C_TWO * (at(1) - at(-2))

    def plus(at):
        return C_ONE * (at(1) - at(0)) + C_TWO * (at(2) - at(-1))

    def along_x(f, x):
        return lambda offset: sx[f, x + 2 + offset]

    def along_y(field):
        return lambda offset: field if offset == 0 else y_at(field, offset)

    def plane(x):
        material = mb[x]
        b = jnp.zeros((cz, ny), jnp.float32)
        for index in range(4):
            b = jnp.where(material == index, BUOY[index], b)
        b = 0.25 * b
        sxy, sxz = sx[1, x + 2], sx[2, x + 2]
        syy, szz, syz = so[0, x], so[1, x], so[2, x]
        out[0, x] = vb[0, x] + b * (
            minus(along_x(0, x)) + minus(along_y(sxy)) + minus(z_at(0, sxz, x))
        )
        out[1, x] = vb[1, x] + b * (
            plus(along_x(1, x)) + plus(along_y(syy)) + minus(z_at(1, syz, x))
        )
        out[2, x] = vb[2, x] + b * (
            plus(along_x(2, x)) + plus(along_y(syz)) + plus(z_at(2, szz, x))
        )

    def step(x, carry):
        plane(x)
        return carry

    lax.fori_loop(2, cx - 2, step, 0)

    for k in range(1, n):
        pack_arrival(k).wait_recv()
    total = recv[0]
    for k in range(1, n):
        total = total + recv[k]
    used = lane_one < cx
    fields = []
    for f in range(4):
        moved = total if f == 0 else pltpu.roll(total, wide - f * cx, 1)
        fields.append(jnp.where(used, moved[:, :128], ownp[f]))
    tau = jnp.zeros((cz, 128), jnp.float32)
    for t in range(tiles):
        moved = pltpu.roll(total, wide - (4 + t) * cx, 1)[:, :128]
        tau = jnp.where(jnp.logical_and(used, my_tile == t), moved, tau)
    for j in range(per):
        picked = jnp.where(lane == 4 * cx + po[me * per + j], total, 0.0)
        tau = jnp.where(lane_one == cx + j, jnp.sum(picked, axis=1, keepdims=True), tau)
    rate = friction(tau + fields[3], fields[0], fields[1], fields[2])
    slip[...] = pltpu.roll(rate, 128 - cx, 1)[:, :per]

    @pl.when(has_left)
    def _():
        for f in range(3):
            x_copy(f, True).wait_recv()

    @pl.when(has_right)
    def _():
        for f in range(3):
            x_copy(f, False).wait_recv()

    def edge(i, carry):
        plane(i + (cx - 4) * (i // 2))
        return carry

    lax.fori_loop(0, 4, edge, 0)

    @pl.when(jnp.logical_and(me >= first_tile, me < first_tile + tiles))
    def _():
        for i in range(cx):
            s = 0.5 * rate[:, i : i + 1]
            low = out[0, i, :, row - 128 : row]
            high = out[0, i, :, row : row + 128]
            middle = 0.5 * (high + pltpu.roll(low, 1, 1))
            out[0, i, :, row : row + 128] = jnp.where(lane_one == 0, middle + s, high)
            out[0, i, :, row - 128 : row] = jnp.where(
                lane_one == 127, pltpu.roll(middle, 127, 1) - s, low
            )

    for k in range(1, n):
        pack_copy(k).wait_send()

    @pl.when(has_above)
    def _():
        for f in range(3):
            z_copy(f, True).wait_send()

    @pl.when(has_below)
    def _():
        for f in range(3):
            z_copy(f, False).wait_send()

    @pl.when(has_right)
    def _():
        for f in range(3):
            x_copy(f, True).wait_send()

    @pl.when(has_left)
    def _():
        for f in range(3):
            x_copy(f, False).wait_send()


def per_device(n, nd, velocity, stress, material, patch_order, fault_params):
    _, cx, cz, ny = stress.shape
    fc = patch_order.shape[0]
    per = fc // n
    wide = -(-(4 * cx + fc + 2) // 128) * 128
    dims = (n, nd, cx, cz, ny, fc, wide)
    tiles = fc // cx
    f32 = jnp.float32
    anywhere = pl.BlockSpec(memory_space=pl.ANY)
    dma = pltpu.SemaphoreType.DMA
    return pl.pallas_call(
        functools.partial(kernel, dims),
        out_shape=(
            jax.ShapeDtypeStruct(velocity.shape, f32),
            jax.ShapeDtypeStruct((cz, per), f32),
        ),
        in_specs=[anywhere, anywhere, anywhere, pl.BlockSpec(memory_space=pltpu.SMEM), anywhere],
        out_specs=(pl.BlockSpec(memory_space=pltpu.VMEM), pl.BlockSpec(memory_space=pltpu.VMEM)),
        scratch_shapes=[
            pltpu.VMEM((3, cx + 4, cz, ny), f32),
            pltpu.VMEM((3, cx, cz, ny), f32),
            pltpu.VMEM((3, cx, cz, ny), f32),
            pltpu.VMEM((cx, cz, ny), jnp.int32),
            pltpu.VMEM((4, cz, per), f32),
            pltpu.VMEM((4, cz, 128), f32),
            pltpu.VMEM((3, cx, 8, ny), f32),
            pltpu.VMEM((3, cx, 8, ny), f32),
            pltpu.VMEM((tiles, cz, wide), f32),
            pltpu.VMEM((n, cz, wide), f32),
            dma((9,)),
            dma((n,)),
            dma((n,)),
            dma((6,)),
            dma((6,)),
            dma((6,)),
            dma((6,)),
        ],
        compiler_params=pltpu.CompilerParams(collective_id=0, has_side_effects=True),
    )(velocity, stress, material, patch_order, fault_params)


def solution(mesh):
    n, nd = mesh.shape["strike"], mesh.shape["depth"]
    return jax.shard_map(
        functools.partial(per_device, n, nd),
        mesh=mesh,
        in_specs=(
            P(None, "strike", "depth", None),
            P(None, "strike", "depth", None),
            P("strike", "depth", None),
            P(),
            P(None, "depth", "strike"),
        ),
        out_specs=(P(None, "strike", "depth", None), P("depth", "strike")),
        check_vma=False,
    )
```

```python
import functools

import jax
import jax.numpy as jnp
from jax import lax
from jax.experimental import pallas as pl
from jax.experimental.pallas import tpu as pltpu
from jax.sharding import PartitionSpec as P

NEWTON = 8
BUOY = (1.0, 0.8, 0.6, 1.25)
C_ONE = 9.0 / 8.0
C_TWO = -1.0 / 24.0
MESH = pl.DeviceIdType.MESH


def inverse_sinh(value):
    magnitude = jnp.log(jnp.abs(value) + jnp.sqrt(1.0 + value * value))
    return jnp.where(value < 0, -magnitude, magnitude)


def friction(tau_total, coef, psi, normal_stress):
    half_q = 0.5 * jnp.exp(psi / coef)
    scale = normal_stress * coef
    rate = jnp.zeros_like(tau_total)
    for _ in range(NEWTON):
        arg_val = rate * half_q
        resid = tau_total - rate - scale * inverse_sinh(arg_val)
        slope = -1.0 - scale * half_q / jnp.sqrt(1.0 + arg_val * arg_val)
        rate = rate - 0.35 * resid / slope
    return rate


def kernel(
    dims, vel, st, mat, po, fp, out, slip,
    sx, so, vb, mb, pb, ownp, zlo, zhi, packs, recv,
    lsem, psend, precv, xsend, xrecv, zsend, zrecv,
):
    n, nd, cx, cz, ny, fc, wide = dims
    row = ny // 2
    per = fc // n
    first_tile = n // 4
    tiles = fc // cx
    me = lax.axis_index("strike")
    dep = lax.axis_index("depth")

    loads = [
        pltpu.make_async_copy(st.at[0], sx.at[0, pl.ds(2, cx)], lsem.at[0]),
        pltpu.make_async_copy(st.at[3], sx.at[1, pl.ds(2, cx)], lsem.at[1]),
        pltpu.make_async_copy(fp, pb, lsem.at[2]),
        pltpu.make_async_copy(st.at[4], sx.at[2, pl.ds(2, cx)], lsem.at[3]),
        pltpu.make_async_copy(st.at[2], so.at[1], lsem.at[4]),
        pltpu.make_async_copy(st.at[5], so.at[2], lsem.at[5]),
        pltpu.make_async_copy(st.at[1], so.at[0], lsem.at[6]),
        pltpu.make_async_copy(mat, mb, lsem.at[7]),
        pltpu.make_async_copy(vel, vb, lsem.at[8]),
    ]
    for load in loads:
        load.start()

    has_left, has_right = me > 0, me < n - 1
    has_below, has_above = dep > 0, dep < nd - 1
    barrier = pltpu.get_barrier_semaphore()
    for k in range(1, n):
        peer = lax.rem(me + k, n)
        pl.semaphore_signal(barrier, inc=1, device_id=(peer, dep), device_id_type=MESH)

    @pl.when(has_below)
    def _():
        pl.semaphore_signal(barrier, inc=1, device_id=(me, dep - 1), device_id_type=MESH)

    @pl.when(has_above)
    def _():
        pl.semaphore_signal(barrier, inc=1, device_id=(me, dep + 1), device_id_type=MESH)

    zero_row = jnp.zeros((2, cz, ny), jnp.float32)

    @pl.when(jnp.logical_not(has_left))
    def _():
        for f in range(3):
            sx[f, 0:2] = zero_row

    @pl.when(jnp.logical_not(has_right))
    def _():
        for f in range(3):
            sx[f, cx + 2 : cx + 4] = zero_row

    @pl.when(jnp.logical_not(has_below))
    def _():
        zlo[...] = jnp.zeros(zlo.shape, jnp.float32)

    @pl.when(jnp.logical_not(has_above))
    def _():
        zhi[...] = jnp.zeros(zhi.shape, jnp.float32)

    lane = lax.broadcasted_iota(jnp.int32, (cz, wide), 1)
    lane_one = lax.broadcasted_iota(jnp.int32, (cz, 128), 1)
    loads[0].wait()
    loads[1].wait()
    loads[2].wait()
    near = jnp.logical_and(me >= first_tile - 1, me <= first_tile + tiles)
    base = jnp.where(near, 4 * cx + (me - first_tile) * cx, -4 * wide)
    normal = jnp.zeros((cz, wide), jnp.float32)
    shear = jnp.zeros((cz, wide), jnp.float32)
    for i in range(cx):
        here = lane == base + i
        normal = jnp.where(here, sx[0, 2 + i, :, row : row + 1], normal)
        shear = jnp.where(here, sx[1, 2 + i, :, row : row + 1], shear)
    dxx = C_ONE * (normal - pltpu.roll(normal, 1, 1)) + C_TWO * (
        pltpu.roll(normal, wide - 1, 1) - pltpu.roll(normal, 2, 1)
    )
    share = shear + 0.5 * dxx
    share = jnp.where(jnp.logical_and(lane >= 4 * cx, lane < 4 * cx + fc), share, 0.0)
    blocks = [share for _ in range(tiles)]
    params = [pb[j].T for j in range(per)]
    for f in range(4):
        mine = jnp.full((cz, 128), 1.0, jnp.float32)
        for j in range(per):
            column = po[me * per + j]
            value = params[j][:, f : f + 1]
            mine = jnp.where(lane_one == cx + j, value, mine)
            for t in range(tiles):
                local = column - t * cx
                held = jnp.logical_and(local >= 0, local < cx)
                place = jnp.where(held, f * cx + local, -1)
                blocks[t] = jnp.where(lane == place, value, blocks[t])
        ownp[f] = mine
    for t in range(tiles):
        packs[t] = blocks[t]
    my_tile = jnp.clip(me - first_tile, 0, tiles - 1)
    recv[me] = packs[my_tile]

    for load in loads[3:6]:
        load.wait()
    pl.semaphore_wait(
        barrier, n - 1 + has_below.astype(jnp.int32) + has_above.astype(jnp.int32)
    )

    def pack_copy(k):
        peer = lax.rem(me + k, n)
        return pltpu.make_async_remote_copy(
            src_ref=packs.at[jnp.clip(peer - first_tile, 0, tiles - 1)],
            dst_ref=recv.at[me],
            send_sem=psend.at[k],
            recv_sem=precv.at[me],
            device_id=(peer, dep),
            device_id_type=MESH,
        )

    def pack_arrival(k):
        source = lax.rem(me + k, n)
        return pltpu.make_async_remote_copy(
            src_ref=packs.at[0],
            dst_ref=recv.at[source],
            send_sem=psend.at[k],
            recv_sem=precv.at[source],
            device_id=(source, dep),
            device_id_type=MESH,
        )

    def x_copy(f, up):
        if up:
            rows = 2 if f == 0 else 1
            src, dst, to = cx + 2 - rows, 2 - rows, me + 1
        else:
            rows = 1 if f == 0 else 2
            src, dst, to = 2, cx + 2, me - 1
        slot = f if up else 3 + f
        return pltpu.make_async_remote_copy(
            src_ref=sx.at[f, pl.ds(src, rows)],
            dst_ref=sx.at[f, pl.ds(dst, rows)],
            send_sem=xsend.at[slot],
            recv_sem=xrecv.at[slot],
            device_id=(to, dep),
            device_id_type=MESH,
        )

    def z_copy(f, up):
        field = (sx.at[2, pl.ds(2, cx)], so.at[2], so.at[1])[f]
        if up:
            rows = 1 if f == 2 else 2
            src, dst, to = cz - rows, zlo.at[f, :, pl.ds(8 - rows, rows)], dep + 1
        else:
            rows = 2 if f == 2 else 1
            src, dst, to = 0, zhi.at[f, :, pl.ds(0, rows)], dep - 1
        slot = f if up else 3 + f
        return pltpu.make_async_remote_copy(
            src_ref=field.at[:, pl.ds(src, rows)],
            dst_ref=dst,
            send_sem=zsend.at[slot],
            recv_sem=zrecv.at[slot],
            device_id=(me, to),
            device_id_type=MESH,
        )

    for k in range(1, n):
        pack_copy(k).start()

    @pl.when(has_above)
    def _():
        for f in range(3):
            z_copy(f, True).start()

    @pl.when(has_below)
    def _():
        for f in range(3):
            z_copy(f, False).start()

    @pl.when(has_right)
    def _():
        for f in range(3):
            x_copy(f, True).start()

    @pl.when(has_left)
    def _():
        for f in range(3):
            x_copy(f, False).start()

    for load in loads[6:]:
        load.wait()

    @pl.when(has_below)
    def _():
        for f in range(3):
            z_copy(f, True).wait_recv()

    @pl.when(has_above)
    def _():
        for f in range(3):
            z_copy(f, False).wait_recv()

    yi = lax.broadcasted_iota(jnp.int32, (cz, ny), 1)

    def y_at(field, offset):
        moved = pltpu.roll(field, (-offset) % ny, 1)
        keep = yi < ny - offset if offset > 0 else yi >= -offset
        return jnp.where(keep, moved, 0.0)

    def z_at(f, field, x):
        joined = jnp.concatenate([zlo[f, x], field, zhi[f, x]], axis=0)
        total = cz + 16
        return lambda offset: pltpu.roll(joined, (-offset) % total, 0)[8 : 8 + cz]

    def minus(at):
        return C_ONE * (at(0) - at(-1)) + C_TWO * (at(1) - at(-2))

    def plus(at):
        return C_ONE * (at(1) - at(0)) + C_TWO * (at(2) - at(-1))

    def along_x(f, x):
        return lambda offset: sx[f, x + 2 + offset]

    def along_y(field):
        return lambda offset: field if offset == 0 else y_at(field, offset)

    def plane(x):
        material = mb[x]
        b = jnp.zeros((cz, ny), jnp.float32)
        for index in range(4):
            b = jnp.where(material == index, BUOY[index], b)
        b = 0.25 * b
        sxy, sxz = sx[1, x + 2], sx[2, x + 2]
        syy, szz, syz = so[0, x], so[1, x], so[2, x]
        out[0, x] = vb[0, x] + b * (
            minus(along_x(0, x)) + minus(along_y(sxy)) + minus(z_at(0, sxz, x))
        )
        out[1, x] = vb[1, x] + b * (
            plus(along_x(1, x)) + plus(along_y(syy)) + minus(z_at(1, syz, x))
        )
        out[2, x] = vb[2, x] + b * (
            plus(along_x(2, x)) + plus(along_y(syz)) + plus(z_at(2, szz, x))
        )

    def step(x, carry):
        plane(x)
        return carry

    lax.fori_loop(2, cx - 2, step, 0)

    for k in range(1, n):
        pack_arrival(k).wait_recv()
    total = recv[0]
    for k in range(1, n):
        total = total + recv[k]
    used = lane_one < cx
    fields = []
    for f in range(4):
        moved = total if f == 0 else pltpu.roll(total, wide - f * cx, 1)
        fields.append(jnp.where(used, moved[:, :128], ownp[f]))
    tau = jnp.zeros((cz, 128), jnp.float32)
    for t in range(tiles):
        moved = pltpu.roll(total, wide - (4 + t) * cx, 1)[:, :128]
        tau = jnp.where(jnp.logical_and(used, my_tile == t), moved, tau)
    for j in range(per):
        picked = jnp.where(lane == 4 * cx + po[me * per + j], total, 0.0)
        tau = jnp.where(lane_one == cx + j, jnp.sum(picked, axis=1, keepdims=True), tau)
    rate = friction(tau + fields[3], fields[0], fields[1], fields[2])
    slip[...] = rate.T[cx : cx + per]

    @pl.when(has_left)
    def _():
        for f in range(3):
            x_copy(f, True).wait_recv()

    @pl.when(has_right)
    def _():
        for f in range(3):
            x_copy(f, False).wait_recv()

    def edge(i, carry):
        plane(i + (cx - 4) * (i // 2))
        return carry

    lax.fori_loop(0, 4, edge, 0)

    @pl.when(jnp.logical_and(me >= first_tile, me < first_tile + tiles))
    def _():
        for i in range(cx):
            s = 0.5 * rate[:, i : i + 1]
            low = out[0, i, :, row - 128 : row]
            high = out[0, i, :, row : row + 128]
            middle = 0.5 * (high + pltpu.roll(low, 1, 1))
            out[0, i, :, row : row + 128] = jnp.where(lane_one == 0, middle + s, high)
            out[0, i, :, row - 128 : row] = jnp.where(
                lane_one == 127, pltpu.roll(middle, 127, 1) - s, low
            )

    for k in range(1, n):
        pack_copy(k).wait_send()

    @pl.when(has_above)
    def _():
        for f in range(3):
            z_copy(f, True).wait_send()

    @pl.when(has_below)
    def _():
        for f in range(3):
            z_copy(f, False).wait_send()

    @pl.when(has_right)
    def _():
        for f in range(3):
            x_copy(f, True).wait_send()

    @pl.when(has_left)
    def _():
        for f in range(3):
            x_copy(f, False).wait_send()


def write_out(held, slip, out, slip_out, sem):
    copies = [pltpu.make_async_copy(slip, slip_out, sem.at[3])]
    copies += [pltpu.make_async_copy(held.at[c], out.at[c], sem.at[c]) for c in range(3)]
    for copy in copies:
        copy.start()
    for copy in copies:
        copy.wait()


def per_device(n, nd, velocity, stress, material, patch_order, fault_params):
    _, cx, cz, ny = stress.shape
    fc = patch_order.shape[0]
    per = fc // n
    wide = -(-(4 * cx + fc + 2) // 128) * 128
    dims = (n, nd, cx, cz, ny, fc, wide)
    tiles = fc // cx
    f32 = jnp.float32
    anywhere = pl.BlockSpec(memory_space=pltpu.HBM)
    dma = pltpu.SemaphoreType.DMA
    held = pl.pallas_call(
        functools.partial(kernel, dims),
        out_shape=(
            jax.ShapeDtypeStruct(velocity.shape, f32),
            jax.ShapeDtypeStruct((per, cz), f32),
        ),
        in_specs=[anywhere, anywhere, anywhere, pl.BlockSpec(memory_space=pltpu.SMEM), anywhere],
        out_specs=(pl.BlockSpec(memory_space=pltpu.VMEM), pl.BlockSpec(memory_space=pltpu.VMEM)),
        scratch_shapes=[
            pltpu.VMEM((3, cx + 4, cz, ny), f32),
            pltpu.VMEM((3, cx, cz, ny), f32),
            pltpu.VMEM((3, cx, cz, ny), f32),
            pltpu.VMEM((cx, cz, ny), jnp.int32),
            pltpu.VMEM((per, 4, cz), f32),
            pltpu.VMEM((4, cz, 128), f32),
            pltpu.VMEM((3, cx, 8, ny), f32),
            pltpu.VMEM((3, cx, 8, ny), f32),
            pltpu.VMEM((tiles, cz, wide), f32),
            pltpu.VMEM((n, cz, wide), f32),
            dma((9,)),
            dma((n,)),
            dma((n,)),
            dma((6,)),
            dma((6,)),
            dma((6,)),
            dma((6,)),
        ],
        compiler_params=pltpu.CompilerParams(collective_id=0, has_side_effects=True, vmem_limit_bytes=12 << 20),
    )(velocity, stress, material, patch_order, jnp.transpose(fault_params, (2, 0, 1)))
    resident = pl.BlockSpec(memory_space=pltpu.VMEM)
    moved, slip = pl.pallas_call(
        write_out,
        out_shape=(
            jax.ShapeDtypeStruct(velocity.shape, f32),
            jax.ShapeDtypeStruct((per, cz), f32),
        ),
        in_specs=[resident, resident],
        out_specs=(anywhere, anywhere),
        scratch_shapes=[dma((4,))],
        compiler_params=pltpu.CompilerParams(vmem_limit_bytes=4 << 20),
    )(*held)
    return moved, slip.T


def solution(mesh):
    n, nd = mesh.shape["strike"], mesh.shape["depth"]
    return jax.shard_map(
        functools.partial(per_device, n, nd),
        mesh=mesh,
        in_specs=(
            P(None, "strike", "depth", None),
            P(None, "strike", "depth", None),
            P("strike", "depth", None),
            P(),
            P(None, "depth", "strike"),
        ),
        out_specs=(P(None, "strike", "depth", None), P("depth", "strike")),
        check_vma=False,
    )
```

```python
import functools

import jax
import jax.numpy as jnp
from jax import lax
from jax.experimental import pallas as pl
from jax.experimental.pallas import tpu as pltpu
from jax.sharding import PartitionSpec as P

NEWTON = 8
BUOY = (1.0, 0.8, 0.6, 1.25)
C_ONE = 9.0 / 8.0
C_TWO = -1.0 / 24.0
MESH = pl.DeviceIdType.MESH


def inverse_sinh(value):
    magnitude = jnp.log(jnp.abs(value) + jnp.sqrt(1.0 + value * value))
    return jnp.where(value < 0, -magnitude, magnitude)


def friction(tau_total, coef, psi, normal_stress):
    half_q = 0.5 * jnp.exp(psi / coef)
    scale = normal_stress * coef
    rate = jnp.zeros_like(tau_total)
    for _ in range(NEWTON):
        arg_val = rate * half_q
        resid = tau_total - rate - scale * inverse_sinh(arg_val)
        slope = -1.0 - scale * half_q / jnp.sqrt(1.0 + arg_val * arg_val)
        rate = rate - 0.35 * resid / slope
    return rate


def kernel(
    dims, vel, st, mat, order, fp, out, slip,
    po, sx, so, vb, mb, pb, ownp, zlo, zhi, packs, recv,
    lsem, psend, precv, xsend, xrecv, zsend, zrecv,
):
    n, nd, cx, cz, ny, fc, wide = dims
    row = ny // 2
    per = fc // n
    first_tile = n // 4
    tiles = fc // cx
    me = lax.axis_index("strike")
    dep = lax.axis_index("depth")

    loads = [
        pltpu.make_async_copy(st.at[0], sx.at[0, pl.ds(2, cx)], lsem.at[0]),
        pltpu.make_async_copy(st.at[3], sx.at[1, pl.ds(2, cx)], lsem.at[1]),
        pltpu.make_async_copy(fp, pb, lsem.at[2]),
        pltpu.make_async_copy(st.at[4], sx.at[2, pl.ds(2, cx)], lsem.at[3]),
        pltpu.make_async_copy(st.at[2], so.at[1], lsem.at[4]),
        pltpu.make_async_copy(st.at[5], so.at[2], lsem.at[5]),
        pltpu.make_async_copy(st.at[1], so.at[0], lsem.at[6]),
        pltpu.make_async_copy(mat, mb, lsem.at[7]),
        pltpu.make_async_copy(vel, vb, lsem.at[8]),
        pltpu.make_async_copy(order, po, lsem.at[9]),
    ]
    for load in loads[9:] + loads[:9]:
        load.start()

    has_left, has_right = me > 0, me < n - 1
    has_below, has_above = dep > 0, dep < nd - 1
    barrier = pltpu.get_barrier_semaphore()
    for k in range(1, n):
        peer = lax.rem(me + k, n)
        pl.semaphore_signal(barrier, inc=1, device_id=(peer, dep), device_id_type=MESH)

    @pl.when(has_below)
    def _():
        pl.semaphore_signal(barrier, inc=1, device_id=(me, dep - 1), device_id_type=MESH)

    @pl.when(has_above)
    def _():
        pl.semaphore_signal(barrier, inc=1, device_id=(me, dep + 1), device_id_type=MESH)

    zero_row = jnp.zeros((2, cz, ny), jnp.float32)

    @pl.when(jnp.logical_not(has_left))
    def _():
        for f in range(3):
            sx[f, 0:2] = zero_row

    @pl.when(jnp.logical_not(has_right))
    def _():
        for f in range(3):
            sx[f, cx + 2 : cx + 4] = zero_row

    @pl.when(jnp.logical_not(has_below))
    def _():
        zlo[...] = jnp.zeros(zlo.shape, jnp.float32)

    @pl.when(jnp.logical_not(has_above))
    def _():
        zhi[...] = jnp.zeros(zhi.shape, jnp.float32)

    lane = lax.broadcasted_iota(jnp.int32, (cz, wide), 1)
    lane_one = lax.broadcasted_iota(jnp.int32, (cz, 128), 1)
    loads[0].wait()
    loads[1].wait()
    loads[2].wait()
    loads[9].wait()
    near = jnp.logical_and(me >= first_tile - 1, me <= first_tile + tiles)
    base = jnp.where(near, 4 * cx + (me - first_tile) * cx, -4 * wide)
    normal = jnp.zeros((cz, wide), jnp.float32)
    shear = jnp.zeros((cz, wide), jnp.float32)
    for i in range(cx):
        here = lane == base + i
        normal = jnp.where(here, sx[0, 2 + i, :, row : row + 1], normal)
        shear = jnp.where(here, sx[1, 2 + i, :, row : row + 1], shear)
    dxx = C_ONE * (normal - pltpu.roll(normal, 1, 1)) + C_TWO * (
        pltpu.roll(normal, wide - 1, 1) - pltpu.roll(normal, 2, 1)
    )
    share = shear + 0.5 * dxx
    share = jnp.where(jnp.logical_and(lane >= 4 * cx, lane < 4 * cx + fc), share, 0.0)
    blocks = [share for _ in range(tiles)]
    params = [pb[j].T for j in range(per)]
    for f in range(4):
        mine = jnp.full((cz, 128), 1.0, jnp.float32)
        for j in range(per):
            column = po[me * per + j]
            value = params[j][:, f : f + 1]
            mine = jnp.where(lane_one == cx + j, value, mine)
            for t in range(tiles):
                local = column - t * cx
                held = jnp.logical_and(local >= 0, local < cx)
                place = jnp.where(held, f * cx + local, -1)
                blocks[t] = jnp.where(lane == place, value, blocks[t])
        ownp[f] = mine
    for t in range(tiles):
        packs[t] = blocks[t]
    my_tile = jnp.clip(me - first_tile, 0, tiles - 1)
    recv[me] = packs[my_tile]

    for load in loads[3:6]:
        load.wait()
    pl.semaphore_wait(
        barrier, n - 1 + has_below.astype(jnp.int32) + has_above.astype(jnp.int32)
    )

    def pack_copy(k):
        peer = lax.rem(me + k, n)
        return pltpu.make_async_remote_copy(
            src_ref=packs.at[jnp.clip(peer - first_tile, 0, tiles - 1)],
            dst_ref=recv.at[me],
            send_sem=psend.at[k],
            recv_sem=precv.at[me],
            device_id=(peer, dep),
            device_id_type=MESH,
        )

    def pack_arrival(k):
        source = lax.rem(me + k, n)
        return pltpu.make_async_remote_copy(
            src_ref=packs.at[0],
            dst_ref=recv.at[source],
            send_sem=psend.at[k],
            recv_sem=precv.at[source],
            device_id=(source, dep),
            device_id_type=MESH,
        )

    def x_copy(f, up):
        if up:
            rows = 2 if f == 0 else 1
            src, dst, to = cx + 2 - rows, 2 - rows, me + 1
        else:
            rows = 1 if f == 0 else 2
            src, dst, to = 2, cx + 2, me - 1
        slot = f if up else 3 + f
        return pltpu.make_async_remote_copy(
            src_ref=sx.at[f, pl.ds(src, rows)],
            dst_ref=sx.at[f, pl.ds(dst, rows)],
            send_sem=xsend.at[slot],
            recv_sem=xrecv.at[slot],
            device_id=(to, dep),
            device_id_type=MESH,
        )

    def z_copy(f, up):
        field = (sx.at[2, pl.ds(2, cx)], so.at[2], so.at[1])[f]
        if up:
            rows = 1 if f == 2 else 2
            src, dst, to = cz - rows, zlo.at[f, :, pl.ds(8 - rows, rows)], dep + 1
        else:
            rows = 2 if f == 2 else 1
            src, dst, to = 0, zhi.at[f, :, pl.ds(0, rows)], dep - 1
        slot = f if up else 3 + f
        return pltpu.make_async_remote_copy(
            src_ref=field.at[:, pl.ds(src, rows)],
            dst_ref=dst,
            send_sem=zsend.at[slot],
            recv_sem=zrecv.at[slot],
            device_id=(me, to),
            device_id_type=MESH,
        )

    for k in range(1, n):
        pack_copy(k).start()

    @pl.when(has_above)
    def _():
        for f in range(3):
            z_copy(f, True).start()

    @pl.when(has_below)
    def _():
        for f in range(3):
            z_copy(f, False).start()

    @pl.when(has_right)
    def _():
        for f in range(3):
            x_copy(f, True).start()

    @pl.when(has_left)
    def _():
        for f in range(3):
            x_copy(f, False).start()

    for load in loads[6:9]:
        load.wait()

    @pl.when(has_below)
    def _():
        for f in range(3):
            z_copy(f, True).wait_recv()

    @pl.when(has_above)
    def _():
        for f in range(3):
            z_copy(f, False).wait_recv()

    yi = lax.broadcasted_iota(jnp.int32, (cz, ny), 1)

    def y_at(field, offset):
        moved = pltpu.roll(field, (-offset) % ny, 1)
        keep = yi < ny - offset if offset > 0 else yi >= -offset
        return jnp.where(keep, moved, 0.0)

    def z_at(f, field, x):
        joined = jnp.concatenate([zlo[f, x], field, zhi[f, x]], axis=0)
        total = cz + 16
        return lambda offset: pltpu.roll(joined, (-offset) % total, 0)[8 : 8 + cz]

    def minus(at):
        return C_ONE * (at(0) - at(-1)) + C_TWO * (at(1) - at(-2))

    def plus(at):
        return C_ONE * (at(1) - at(0)) + C_TWO * (at(2) - at(-1))

    def along_x(f, x):
        return lambda offset: sx[f, x + 2 + offset]

    def along_y(field):
        return lambda offset: field if offset == 0 else y_at(field, offset)

    def plane(x):
        material = mb[x]
        b = jnp.zeros((cz, ny), jnp.float32)
        for index in range(4):
            b = jnp.where(material == index, BUOY[index], b)
        b = 0.25 * b
        sxy, sxz = sx[1, x + 2], sx[2, x + 2]
        syy, szz, syz = so[0, x], so[1, x], so[2, x]
        out[0, x] = vb[0, x] + b * (
            minus(along_x(0, x)) + minus(along_y(sxy)) + minus(z_at(0, sxz, x))
        )
        out[1, x] = vb[1, x] + b * (
            plus(along_x(1, x)) + plus(along_y(syy)) + minus(z_at(1, syz, x))
        )
        out[2, x] = vb[2, x] + b * (
            plus(along_x(2, x)) + plus(along_y(syz)) + plus(z_at(2, szz, x))
        )

    def step(x, carry):
        plane(x)
        return carry

    lax.fori_loop(2, cx - 2, step, 0)

    for k in range(1, n):
        pack_arrival(k).wait_recv()
    total = recv[0]
    for k in range(1, n):
        total = total + recv[k]
    used = lane_one < cx
    fields = []
    for f in range(4):
        moved = total if f == 0 else pltpu.roll(total, wide - f * cx, 1)
        fields.append(jnp.where(used, moved[:, :128], ownp[f]))
    tau = jnp.zeros((cz, 128), jnp.float32)
    for t in range(tiles):
        moved = pltpu.roll(total, wide - (4 + t) * cx, 1)[:, :128]
        tau = jnp.where(jnp.logical_and(used, my_tile == t), moved, tau)
    for j in range(per):
        picked = jnp.where(lane == 4 * cx + po[me * per + j], total, 0.0)
        tau = jnp.where(lane_one == cx + j, jnp.sum(picked, axis=1, keepdims=True), tau)
    rate = friction(tau + fields[3], fields[0], fields[1], fields[2])
    slip[...] = rate.T[cx : cx + per]

    @pl.when(has_left)
    def _():
        for f in range(3):
            x_copy(f, True).wait_recv()

    @pl.when(has_right)
    def _():
        for f in range(3):
            x_copy(f, False).wait_recv()

    def edge(i, carry):
        plane(i + (cx - 4) * (i // 2))
        return carry

    lax.fori_loop(0, 4, edge, 0)

    @pl.when(jnp.logical_and(me >= first_tile, me < first_tile + tiles))
    def _():
        for i in range(cx):
            s = 0.5 * rate[:, i : i + 1]
            low = out[0, i, :, row - 128 : row]
            high = out[0, i, :, row : row + 128]
            middle = 0.5 * (high + pltpu.roll(low, 1, 1))
            out[0, i, :, row : row + 128] = jnp.where(lane_one == 0, middle + s, high)
            out[0, i, :, row - 128 : row] = jnp.where(
                lane_one == 127, pltpu.roll(middle, 127, 1) - s, low
            )

    for k in range(1, n):
        pack_copy(k).wait_send()

    @pl.when(has_above)
    def _():
        for f in range(3):
            z_copy(f, True).wait_send()

    @pl.when(has_below)
    def _():
        for f in range(3):
            z_copy(f, False).wait_send()

    @pl.when(has_right)
    def _():
        for f in range(3):
            x_copy(f, True).wait_send()

    @pl.when(has_left)
    def _():
        for f in range(3):
            x_copy(f, False).wait_send()


def write_out(held, slip, out, slip_out, sem):
    copies = [pltpu.make_async_copy(slip, slip_out, sem.at[3])]
    copies += [pltpu.make_async_copy(held.at[c], out.at[c], sem.at[c]) for c in range(3)]
    for copy in copies:
        copy.start()
    for copy in copies:
        copy.wait()


def per_device(n, nd, velocity, stress, material, patch_order, fault_params):
    _, cx, cz, ny = stress.shape
    fc = patch_order.shape[0]
    per = fc // n
    wide = -(-(4 * cx + fc + 2) // 128) * 128
    dims = (n, nd, cx, cz, ny, fc, wide)
    tiles = fc // cx
    f32 = jnp.float32
    anywhere = pl.BlockSpec(memory_space=pltpu.HBM)
    dma = pltpu.SemaphoreType.DMA
    params = jnp.transpose(fault_params, (2, 0, 1))
    big = (velocity, stress, material, patch_order, params)
    held = pl.pallas_call(
        functools.partial(kernel, dims),
        out_shape=(
            jax.ShapeDtypeStruct(velocity.shape, f32),
            jax.ShapeDtypeStruct((per, cz), f32),
        ),
        in_specs=[anywhere] * 5,
        out_specs=(pl.BlockSpec(memory_space=pltpu.VMEM), pl.BlockSpec(memory_space=pltpu.VMEM)),
        scratch_shapes=[
            pltpu.SMEM((fc,), jnp.int32),
            pltpu.VMEM((3, cx + 4, cz, ny), f32),
            pltpu.VMEM((3, cx, cz, ny), f32),
            pltpu.VMEM((3, cx, cz, ny), f32),
            pltpu.VMEM((cx, cz, ny), jnp.int32),
            pltpu.VMEM((per, 4, cz), f32),
            pltpu.VMEM((4, cz, 128), f32),
            pltpu.VMEM((3, cx, 8, ny), f32),
            pltpu.VMEM((3, cx, 8, ny), f32),
            pltpu.VMEM((tiles, cz, wide), f32),
            pltpu.VMEM((n, cz, wide), f32),
            dma((10,)),
            dma((n,)),
            dma((n,)),
            dma((6,)),
            dma((6,)),
            dma((6,)),
            dma((6,)),
        ],
        compiler_params=pltpu.CompilerParams(collective_id=0, has_side_effects=True, vmem_limit_bytes=12 << 20),
    )(*[pltpu.with_memory_space_constraint(v, pltpu.HBM) for v in big])
    resident = pl.BlockSpec(memory_space=pltpu.VMEM)
    moved, slip = pl.pallas_call(
        write_out,
        out_shape=(
            jax.ShapeDtypeStruct(velocity.shape, f32),
            jax.ShapeDtypeStruct((per, cz), f32),
        ),
        in_specs=[resident, resident],
        out_specs=(anywhere, anywhere),
        scratch_shapes=[dma((4,))],
        compiler_params=pltpu.CompilerParams(vmem_limit_bytes=4 << 20),
    )(*held)
    return moved, slip.T


def solution(mesh):
    n, nd = mesh.shape["strike"], mesh.shape["depth"]
    return jax.shard_map(
        functools.partial(per_device, n, nd),
        mesh=mesh,
        in_specs=(
            P(None, "strike", "depth", None),
            P(None, "strike", "depth", None),
            P("strike", "depth", None),
            P(),
            P(None, "depth", "strike"),
        ),
        out_specs=(P(None, "strike", "depth", None), P("depth", "strike")),
        check_vma=False,
    )
```

```python
import functools

import jax
import jax.numpy as jnp
from jax import lax
from jax.experimental import pallas as pl
from jax.experimental.pallas import tpu as pltpu
from jax.sharding import PartitionSpec as P

NEWTON = 8
BUOY = (1.0, 0.8, 0.6, 1.25)
C_ONE = 9.0 / 8.0
C_TWO = -1.0 / 24.0
MESH = pl.DeviceIdType.MESH


def friction(tau_total, coef, psi, normal_stress):
    half_q = 0.5 * jnp.exp(psi / coef)
    scale = normal_stress * coef
    stiff = scale * half_q
    rate = jnp.zeros_like(tau_total)
    for _ in range(NEWTON):
        arg_val = rate * half_q
        root = jnp.sqrt(1.0 + arg_val * arg_val)
        magnitude = jnp.log(jnp.abs(arg_val) + root)
        resid = tau_total - rate - scale * jnp.where(arg_val < 0, -magnitude, magnitude)
        rate = rate + 0.35 * resid * (root / (root + stiff))
    return rate


def kernel(
    dims, vel, st, mat, order, fp, out, slip,
    po, sx, so, vb, mb, pb, ownp, zlo, zhi, packs, recv,
    lsem, psend, precv, xsend, xrecv, zsend, zrecv,
):
    n, nd, cx, cz, ny, fc, wide = dims
    row = ny // 2
    per = fc // n
    first_tile = n // 4
    tiles = fc // cx
    me = lax.axis_index("strike")
    dep = lax.axis_index("depth")

    loads = [
        pltpu.make_async_copy(st.at[0], sx.at[0, pl.ds(2, cx)], lsem.at[0]),
        pltpu.make_async_copy(st.at[3], sx.at[1, pl.ds(2, cx)], lsem.at[1]),
        pltpu.make_async_copy(fp, pb, lsem.at[2]),
        pltpu.make_async_copy(st.at[4], sx.at[2, pl.ds(2, cx)], lsem.at[3]),
        pltpu.make_async_copy(st.at[2], so.at[1], lsem.at[4]),
        pltpu.make_async_copy(st.at[5], so.at[2], lsem.at[5]),
        pltpu.make_async_copy(st.at[1], so.at[0], lsem.at[6]),
        pltpu.make_async_copy(mat, mb, lsem.at[7]),
        pltpu.make_async_copy(vel, vb, lsem.at[8]),
        pltpu.make_async_copy(order, po, lsem.at[9]),
    ]
    has_left, has_right = me > 0, me < n - 1
    has_below, has_above = dep > 0, dep < nd - 1
    barrier = pltpu.get_barrier_semaphore()
    for k in range(1, n):
        peer = lax.rem(me + k, n)
        pl.semaphore_signal(barrier, inc=1, device_id=(peer, dep), device_id_type=MESH)

    @pl.when(has_below)
    def _():
        pl.semaphore_signal(barrier, inc=1, device_id=(me, dep - 1), device_id_type=MESH)

    @pl.when(has_above)
    def _():
        pl.semaphore_signal(barrier, inc=1, device_id=(me, dep + 1), device_id_type=MESH)

    for load in loads[9:] + loads[:9]:
        load.start()

    zero_row = jnp.zeros((2, cz, ny), jnp.float32)

    @pl.when(jnp.logical_not(has_left))
    def _():
        for f in range(3):
            sx[f, 0:2] = zero_row

    @pl.when(jnp.logical_not(has_right))
    def _():
        for f in range(3):
            sx[f, cx + 2 : cx + 4] = zero_row

    @pl.when(jnp.logical_not(has_below))
    def _():
        zlo[...] = jnp.zeros(zlo.shape, jnp.float32)

    @pl.when(jnp.logical_not(has_above))
    def _():
        zhi[...] = jnp.zeros(zhi.shape, jnp.float32)

    lane = lax.broadcasted_iota(jnp.int32, (cz, wide), 1)
    lane_one = lax.broadcasted_iota(jnp.int32, (cz, 128), 1)
    loads[0].wait()
    loads[1].wait()
    loads[2].wait()
    loads[9].wait()
    near = jnp.logical_and(me >= first_tile - 1, me <= first_tile + tiles)
    base = jnp.where(near, 4 * cx + (me - first_tile) * cx, -4 * wide)
    normal = jnp.zeros((cz, wide), jnp.float32)
    shear = jnp.zeros((cz, wide), jnp.float32)
    for i in range(cx):
        here = lane == base + i
        normal = jnp.where(here, sx[0, 2 + i, :, row : row + 1], normal)
        shear = jnp.where(here, sx[1, 2 + i, :, row : row + 1], shear)
    dxx = C_ONE * (normal - pltpu.roll(normal, 1, 1)) + C_TWO * (
        pltpu.roll(normal, wide - 1, 1) - pltpu.roll(normal, 2, 1)
    )
    share = shear + 0.5 * dxx
    share = jnp.where(jnp.logical_and(lane >= 4 * cx, lane < 4 * cx + fc), share, 0.0)
    blocks = [share for _ in range(tiles)]
    params = [pb[j].T for j in range(per)]
    for f in range(4):
        mine = jnp.full((cz, 128), 1.0, jnp.float32)
        for j in range(per):
            column = po[me * per + j]
            value = params[j][:, f : f + 1]
            mine = jnp.where(lane_one == cx + j, value, mine)
            for t in range(tiles):
                local = column - t * cx
                held = jnp.logical_and(local >= 0, local < cx)
                place = jnp.where(held, f * cx + local, -1)
                blocks[t] = jnp.where(lane == place, value, blocks[t])
        ownp[f] = mine
    for t in range(tiles):
        packs[t] = blocks[t]
    my_tile = jnp.clip(me - first_tile, 0, tiles - 1)
    recv[me] = packs[my_tile]

    for load in loads[3:6]:
        load.wait()
    pl.semaphore_wait(
        barrier, n - 1 + has_below.astype(jnp.int32) + has_above.astype(jnp.int32)
    )

    def pack_copy(k):
        peer = lax.rem(me + k, n)
        return pltpu.make_async_remote_copy(
            src_ref=packs.at[jnp.clip(peer - first_tile, 0, tiles - 1)],
            dst_ref=recv.at[me],
            send_sem=psend.at[k],
            recv_sem=precv.at[me],
            device_id=(peer, dep),
            device_id_type=MESH,
        )

    def pack_arrival(k):
        source = lax.rem(me + k, n)
        return pltpu.make_async_remote_copy(
            src_ref=packs.at[0],
            dst_ref=recv.at[source],
            send_sem=psend.at[k],
            recv_sem=precv.at[source],
            device_id=(source, dep),
            device_id_type=MESH,
        )

    def x_copy(f, up):
        if up:
            rows = 2 if f == 0 else 1
            src, dst, to = cx + 2 - rows, 2 - rows, me + 1
        else:
            rows = 1 if f == 0 else 2
            src, dst, to = 2, cx + 2, me - 1
        slot = f if up else 3 + f
        return pltpu.make_async_remote_copy(
            src_ref=sx.at[f, pl.ds(src, rows)],
            dst_ref=sx.at[f, pl.ds(dst, rows)],
            send_sem=xsend.at[slot],
            recv_sem=xrecv.at[slot],
            device_id=(to, dep),
            device_id_type=MESH,
        )

    def z_copy(f, up):
        field = (sx.at[2, pl.ds(2, cx)], so.at[2], so.at[1])[f]
        if up:
            rows = 1 if f == 2 else 2
            src, dst, to = cz - rows, zlo.at[f, :, pl.ds(8 - rows, rows)], dep + 1
        else:
            rows = 2 if f == 2 else 1
            src, dst, to = 0, zhi.at[f, :, pl.ds(0, rows)], dep - 1
        slot = f if up else 3 + f
        return pltpu.make_async_remote_copy(
            src_ref=field.at[:, pl.ds(src, rows)],
            dst_ref=dst,
            send_sem=zsend.at[slot],
            recv_sem=zrecv.at[slot],
            device_id=(me, to),
            device_id_type=MESH,
        )

    for k in range(1, n):
        pack_copy(k).start()

    @pl.when(has_above)
    def _():
        for f in range(3):
            z_copy(f, True).start()

    @pl.when(has_below)
    def _():
        for f in range(3):
            z_copy(f, False).start()

    @pl.when(has_right)
    def _():
        for f in range(3):
            x_copy(f, True).start()

    @pl.when(has_left)
    def _():
        for f in range(3):
            x_copy(f, False).start()

    for load in loads[6:9]:
        load.wait()

    yi = lax.broadcasted_iota(jnp.int32, (cz, ny), 1)

    def y_at(field, offset):
        moved = pltpu.roll(field, (-offset) % ny, 1)
        keep = yi < ny - offset if offset > 0 else yi >= -offset
        return jnp.where(keep, moved, 0.0)

    blank = jnp.zeros((8, ny), jnp.float32)

    def z_at(f, field, x, faces):
        ends = (zlo[f, x], zhi[f, x]) if faces else (blank, blank)
        joined = jnp.concatenate([ends[0], field, ends[1]], axis=0)
        total = cz + 16
        return lambda offset: pltpu.roll(joined, (-offset) % total, 0)[8 : 8 + cz]

    def minus(at):
        return C_ONE * (at(0) - at(-1)) + C_TWO * (at(1) - at(-2))

    def plus(at):
        return C_ONE * (at(1) - at(0)) + C_TWO * (at(2) - at(-1))

    def along_x(f, x):
        return lambda offset: sx[f, x + 2 + offset]

    def along_y(field):
        return lambda offset: field if offset == 0 else y_at(field, offset)

    def buoyancy(x):
        material = mb[x]
        b = jnp.zeros((cz, ny), jnp.float32)
        for index in range(4):
            b = jnp.where(material == index, BUOY[index], b)
        return 0.25 * b

    def plane(x, faces):
        b = buoyancy(x)
        sxy, sxz = sx[1, x + 2], sx[2, x + 2]
        syy, szz, syz = so[0, x], so[1, x], so[2, x]
        out[0, x] = vb[0, x] + b * (
            minus(along_x(0, x)) + minus(along_y(sxy)) + minus(z_at(0, sxz, x, faces))
        )
        out[1, x] = vb[1, x] + b * (
            plus(along_x(1, x)) + plus(along_y(syy)) + minus(z_at(1, syz, x, faces))
        )
        out[2, x] = vb[2, x] + b * (
            plus(along_x(2, x)) + plus(along_y(syz)) + plus(z_at(2, szz, x, faces))
        )

    def step(x, carry):
        plane(x, False)
        return carry

    lax.fori_loop(2, cx - 2, step, 0)

    @pl.when(has_below)
    def _():
        for f in range(3):
            z_copy(f, True).wait_recv()

    @pl.when(has_above)
    def _():
        for f in range(3):
            z_copy(f, False).wait_recv()

    def face(x, carry):
        b = buoyancy(x)
        nothing = jnp.zeros((cz, ny), jnp.float32)
        out[0, x] += b * minus(z_at(0, nothing, x, True))
        out[1, x] += b * minus(z_at(1, nothing, x, True))
        out[2, x] += b * plus(z_at(2, nothing, x, True))
        return carry

    lax.fori_loop(2, cx - 2, face, 0)

    for k in range(1, n):
        pack_arrival(k).wait_recv()
    total = recv[0]
    for k in range(1, n):
        total = total + recv[k]
    used = lane_one < cx
    fields = []
    for f in range(4):
        moved = total if f == 0 else pltpu.roll(total, wide - f * cx, 1)
        fields.append(jnp.where(used, moved[:, :128], ownp[f]))
    tau = jnp.zeros((cz, 128), jnp.float32)
    for t in range(tiles):
        moved = pltpu.roll(total, wide - (4 + t) * cx, 1)[:, :128]
        tau = jnp.where(jnp.logical_and(used, my_tile == t), moved, tau)
    for j in range(per):
        picked = jnp.where(lane == 4 * cx + po[me * per + j], total, 0.0)
        tau = jnp.where(lane_one == cx + j, jnp.sum(picked, axis=1, keepdims=True), tau)
    rate = friction(tau + fields[3], fields[0], fields[1], fields[2])
    slip[...] = rate.T[cx : cx + per]

    @pl.when(has_left)
    def _():
        for f in range(3):
            x_copy(f, True).wait_recv()

    @pl.when(has_right)
    def _():
        for f in range(3):
            x_copy(f, False).wait_recv()

    def edge(i, carry):
        plane(i + (cx - 4) * (i // 2), True)
        return carry

    lax.fori_loop(0, 4, edge, 0)

    @pl.when(jnp.logical_and(me >= first_tile, me < first_tile + tiles))
    def _():
        for i in range(cx):
            s = 0.5 * rate[:, i : i + 1]
            low = out[0, i, :, row - 128 : row]
            high = out[0, i, :, row : row + 128]
            middle = 0.5 * (high + pltpu.roll(low, 1, 1))
            out[0, i, :, row : row + 128] = jnp.where(lane_one == 0, middle + s, high)
            out[0, i, :, row - 128 : row] = jnp.where(
                lane_one == 127, pltpu.roll(middle, 127, 1) - s, low
            )

    for k in range(1, n):
        pack_copy(k).wait_send()

    @pl.when(has_above)
    def _():
        for f in range(3):
            z_copy(f, True).wait_send()

    @pl.when(has_below)
    def _():
        for f in range(3):
            z_copy(f, False).wait_send()

    @pl.when(has_right)
    def _():
        for f in range(3):
            x_copy(f, True).wait_send()

    @pl.when(has_left)
    def _():
        for f in range(3):
            x_copy(f, False).wait_send()


def write_out(held, slip, out, slip_out, sem):
    copies = [pltpu.make_async_copy(slip, slip_out, sem.at[3])]
    copies += [pltpu.make_async_copy(held.at[c], out.at[c], sem.at[c]) for c in range(3)]
    for copy in copies:
        copy.start()
    for copy in copies:
        copy.wait()


def per_device(n, nd, velocity, stress, material, patch_order, fault_params):
    _, cx, cz, ny = stress.shape
    fc = patch_order.shape[0]
    per = fc // n
    wide = -(-(4 * cx + fc + 2) // 128) * 128
    dims = (n, nd, cx, cz, ny, fc, wide)
    tiles = fc // cx
    f32 = jnp.float32
    anywhere = pl.BlockSpec(memory_space=pltpu.HBM)
    dma = pltpu.SemaphoreType.DMA
    params = jnp.transpose(fault_params, (2, 0, 1))
    big = (velocity, stress, material, patch_order, params)
    held = pl.pallas_call(
        functools.partial(kernel, dims),
        out_shape=(
            jax.ShapeDtypeStruct(velocity.shape, f32),
            jax.ShapeDtypeStruct((per, cz), f32),
        ),
        in_specs=[anywhere] * 5,
        out_specs=(pl.BlockSpec(memory_space=pltpu.VMEM), pl.BlockSpec(memory_space=pltpu.VMEM)),
        scratch_shapes=[
            pltpu.SMEM((fc,), jnp.int32),
            pltpu.VMEM((3, cx + 4, cz, ny), f32),
            pltpu.VMEM((3, cx, cz, ny), f32),
            pltpu.VMEM((3, cx, cz, ny), f32),
            pltpu.VMEM((cx, cz, ny), jnp.int32),
            pltpu.VMEM((per, 4, cz), f32),
            pltpu.VMEM((4, cz, 128), f32),
            pltpu.VMEM((3, cx, 8, ny), f32),
            pltpu.VMEM((3, cx, 8, ny), f32),
            pltpu.VMEM((tiles, cz, wide), f32),
            pltpu.VMEM((n, cz, wide), f32),
            dma((10,)),
            dma((n,)),
            dma((n,)),
            dma((6,)),
            dma((6,)),
            dma((6,)),
            dma((6,)),
        ],
        compiler_params=pltpu.CompilerParams(collective_id=0, has_side_effects=True, vmem_limit_bytes=12 << 20),
    )(*[pltpu.with_memory_space_constraint(v, pltpu.HBM) for v in big])
    resident = pl.BlockSpec(memory_space=pltpu.VMEM)
    moved, slip = pl.pallas_call(
        write_out,
        out_shape=(
            jax.ShapeDtypeStruct(velocity.shape, f32),
            jax.ShapeDtypeStruct((per, cz), f32),
        ),
        in_specs=[resident, resident],
        out_specs=(anywhere, anywhere),
        scratch_shapes=[dma((4,))],
        compiler_params=pltpu.CompilerParams(vmem_limit_bytes=4 << 20),
    )(*held)
    return moved, slip.T


def solution(mesh):
    n, nd = mesh.shape["strike"], mesh.shape["depth"]
    return jax.shard_map(
        functools.partial(per_device, n, nd),
        mesh=mesh,
        in_specs=(
            P(None, "strike", "depth", None),
            P(None, "strike", "depth", None),
            P("strike", "depth", None),
            P(),
            P(None, "depth", "strike"),
        ),
        out_specs=(P(None, "strike", "depth", None), P("depth", "strike")),
        check_vma=False,
    )
```

```python
import functools

import jax
import jax.numpy as jnp
from jax import lax
from jax.experimental import pallas as pl
from jax.experimental.pallas import tpu as pltpu
from jax.sharding import PartitionSpec as P

NEWTON = 8
BUOY = (1.0, 0.8, 0.6, 1.25)
C_ONE = 9.0 / 8.0
C_TWO = -1.0 / 24.0
MESH = pl.DeviceIdType.MESH


def friction(tau_total, coef, psi, normal_stress):
    half_q = 0.5 * jnp.exp(psi / coef)
    scale = normal_stress * coef
    stiff = scale * half_q
    rate = jnp.zeros_like(tau_total)
    for _ in range(NEWTON):
        arg_val = rate * half_q
        root = jnp.sqrt(1.0 + arg_val * arg_val)
        magnitude = jnp.log(jnp.abs(arg_val) + root)
        resid = tau_total - rate - scale * jnp.where(arg_val < 0, -magnitude, magnitude)
        rate = rate + 0.35 * resid * (root / (root + stiff))
    return rate


def kernel(
    dims, vel, st, mat, order, fp, out, slip,
    po, sx, so, vb, mb, pb, ownp, zlo, zhi, packs, recv,
    lsem, psend, precv, xsend, xrecv, zsend, zrecv,
):
    n, nd, cx, cz, ny, fc, wide = dims
    row = ny // 2
    per = fc // n
    first_tile = n // 4
    tiles = fc // cx
    me = lax.axis_index("strike")
    dep = lax.axis_index("depth")

    loads = [
        pltpu.make_async_copy(st.at[0], sx.at[0, pl.ds(2, cx)], lsem.at[0]),
        pltpu.make_async_copy(st.at[3], sx.at[1, pl.ds(2, cx)], lsem.at[1]),
        pltpu.make_async_copy(fp, pb, lsem.at[2]),
        pltpu.make_async_copy(st.at[4], sx.at[2, pl.ds(2, cx)], lsem.at[3]),
        pltpu.make_async_copy(st.at[2], so.at[1], lsem.at[4]),
        pltpu.make_async_copy(st.at[5], so.at[2], lsem.at[5]),
        pltpu.make_async_copy(st.at[1], so.at[0], lsem.at[6]),
        pltpu.make_async_copy(mat, mb, lsem.at[7]),
        pltpu.make_async_copy(vel, vb, lsem.at[8]),
        pltpu.make_async_copy(order, po, lsem.at[9]),
    ]
    has_left, has_right = me > 0, me < n - 1
    has_below, has_above = dep > 0, dep < nd - 1
    barrier = pltpu.get_barrier_semaphore()
    for k in range(1, n):
        peer = lax.rem(me + k, n)
        pl.semaphore_signal(barrier, inc=1, device_id=(peer, dep), device_id_type=MESH)

    @pl.when(has_below)
    def _():
        pl.semaphore_signal(barrier, inc=1, device_id=(me, dep - 1), device_id_type=MESH)

    @pl.when(has_above)
    def _():
        pl.semaphore_signal(barrier, inc=1, device_id=(me, dep + 1), device_id_type=MESH)

    for load in loads[9:] + loads[:9]:
        load.start()

    zero_row = jnp.zeros((2, cz, ny), jnp.float32)

    @pl.when(jnp.logical_not(has_left))
    def _():
        for f in range(3):
            sx[f, 0:2] = zero_row

    @pl.when(jnp.logical_not(has_right))
    def _():
        for f in range(3):
            sx[f, cx + 2 : cx + 4] = zero_row

    @pl.when(jnp.logical_not(has_below))
    def _():
        zlo[...] = jnp.zeros(zlo.shape, jnp.float32)

    @pl.when(jnp.logical_not(has_above))
    def _():
        zhi[...] = jnp.zeros(zhi.shape, jnp.float32)

    lane = lax.broadcasted_iota(jnp.int32, (cz, wide), 1)
    lane_one = lax.broadcasted_iota(jnp.int32, (cz, 128), 1)
    loads[0].wait()
    loads[1].wait()
    loads[2].wait()
    loads[9].wait()
    near = jnp.logical_and(me >= first_tile - 1, me <= first_tile + tiles)
    base = jnp.where(near, 4 * cx + (me - first_tile) * cx, -4 * wide)
    normal = jnp.zeros((cz, wide), jnp.float32)
    shear = jnp.zeros((cz, wide), jnp.float32)
    for i in range(cx):
        here = lane == base + i
        normal = jnp.where(here, sx[0, 2 + i, :, row : row + 1], normal)
        shear = jnp.where(here, sx[1, 2 + i, :, row : row + 1], shear)
    dxx = C_ONE * (normal - pltpu.roll(normal, 1, 1)) + C_TWO * (
        pltpu.roll(normal, wide - 1, 1) - pltpu.roll(normal, 2, 1)
    )
    share = shear + 0.5 * dxx
    share = jnp.where(jnp.logical_and(lane >= 4 * cx, lane < 4 * cx + fc), share, 0.0)
    blocks = [share for _ in range(tiles)]
    params = [pb[j].T for j in range(per)]
    for f in range(4):
        mine = jnp.full((cz, 128), 1.0, jnp.float32)
        for j in range(per):
            column = po[me * per + j]
            value = params[j][:, f : f + 1]
            mine = jnp.where(lane_one == cx + j, value, mine)
            for t in range(tiles):
                local = column - t * cx
                held = jnp.logical_and(local >= 0, local < cx)
                place = jnp.where(held, f * cx + local, -1)
                blocks[t] = jnp.where(lane == place, value, blocks[t])
        ownp[f] = mine
    for t in range(tiles):
        packs[t] = blocks[t]
    my_tile = jnp.clip(me - first_tile, 0, tiles - 1)
    recv[me] = packs[my_tile]

    for load in loads[3:6]:
        load.wait()
    pl.semaphore_wait(
        barrier, n - 1 + has_below.astype(jnp.int32) + has_above.astype(jnp.int32)
    )

    def pack_copy(k):
        peer = lax.rem(me + k, n)
        return pltpu.make_async_remote_copy(
            src_ref=packs.at[jnp.clip(peer - first_tile, 0, tiles - 1)],
            dst_ref=recv.at[me],
            send_sem=psend.at[k],
            recv_sem=precv.at[me],
            device_id=(peer, dep),
            device_id_type=MESH,
        )

    def pack_arrival(k):
        source = lax.rem(me + k, n)
        return pltpu.make_async_remote_copy(
            src_ref=packs.at[0],
            dst_ref=recv.at[source],
            send_sem=psend.at[k],
            recv_sem=precv.at[source],
            device_id=(source, dep),
            device_id_type=MESH,
        )

    def x_copy(f, up):
        if up:
            rows = 2 if f == 0 else 1
            src, dst, to = cx + 2 - rows, 2 - rows, me + 1
        else:
            rows = 1 if f == 0 else 2
            src, dst, to = 2, cx + 2, me - 1
        slot = f if up else 3 + f
        return pltpu.make_async_remote_copy(
            src_ref=sx.at[f, pl.ds(src, rows)],
            dst_ref=sx.at[f, pl.ds(dst, rows)],
            send_sem=xsend.at[slot],
            recv_sem=xrecv.at[slot],
            device_id=(to, dep),
            device_id_type=MESH,
        )

    def z_copy(f, up):
        field = (sx.at[2, pl.ds(2, cx)], so.at[2], so.at[1])[f]
        if up:
            rows = 1 if f == 2 else 2
            src, dst, to = cz - rows, zlo.at[f, :, pl.ds(8 - rows, rows)], dep + 1
        else:
            rows = 2 if f == 2 else 1
            src, dst, to = 0, zhi.at[f, :, pl.ds(0, rows)], dep - 1
        slot = f if up else 3 + f
        return pltpu.make_async_remote_copy(
            src_ref=field.at[:, pl.ds(src, rows)],
            dst_ref=dst,
            send_sem=zsend.at[slot],
            recv_sem=zrecv.at[slot],
            device_id=(me, to),
            device_id_type=MESH,
        )

    for k in range(1, n):
        pack_copy(k).start()

    @pl.when(has_above)
    def _():
        for f in range(3):
            z_copy(f, True).start()

    @pl.when(has_below)
    def _():
        for f in range(3):
            z_copy(f, False).start()

    @pl.when(has_right)
    def _():
        for f in range(3):
            x_copy(f, True).start()

    @pl.when(has_left)
    def _():
        for f in range(3):
            x_copy(f, False).start()

    for load in loads[6:9]:
        load.wait()

    yi = lax.broadcasted_iota(jnp.int32, (cz, ny), 1)

    def y_at(field, offset):
        moved = pltpu.roll(field, (-offset) % ny, 1)
        keep = yi < ny - offset if offset > 0 else yi >= -offset
        return jnp.where(keep, moved, 0.0)

    blank = jnp.zeros((8, ny), jnp.float32)

    def z_at(f, field, x, faces):
        ends = (zlo[f, x], zhi[f, x]) if faces else (blank, blank)
        joined = jnp.concatenate([ends[0], field, ends[1]], axis=0)
        total = cz + 16
        return lambda offset: pltpu.roll(joined, (-offset) % total, 0)[8 : 8 + cz]

    def minus(at):
        return C_ONE * (at(0) - at(-1)) + C_TWO * (at(1) - at(-2))

    def plus(at):
        return C_ONE * (at(1) - at(0)) + C_TWO * (at(2) - at(-1))

    def along_x(f, x):
        return lambda offset: sx[f, x + 2 + offset]

    def along_y(field):
        return lambda offset: field if offset == 0 else y_at(field, offset)

    def buoyancy(x):
        material = mb[x]
        b = jnp.zeros((cz, ny), jnp.float32)
        for index in range(4):
            b = jnp.where(material == index, BUOY[index], b)
        return 0.25 * b

    def across(x):
        return minus(along_x(0, x)), plus(along_x(1, x)), plus(along_x(2, x))

    def local(x):
        sxz, szz, syz = sx[2, x + 2], so[1, x], so[2, x]
        return (
            minus(along_y(sx[1, x + 2])) + minus(z_at(0, sxz, x, False)),
            plus(along_y(so[0, x])) + minus(z_at(1, syz, x, False)),
            plus(along_y(syz)) + plus(z_at(2, szz, x, False)),
        )

    def inner(x, carry):
        b, along, rest = buoyancy(x), across(x), local(x)
        for c in range(3):
            out[c, x] = vb[c, x] + b * (along[c] + rest[c])
        return carry

    def outer(x):
        b, rest = buoyancy(x), local(x)
        for c in range(3):
            out[c, x] = vb[c, x] + b * rest[c]

    edges = (0, 1, cx - 2, cx - 1)
    lax.fori_loop(2, cx - 2, inner, 0)
    for x in edges:
        outer(x)

    @pl.when(has_below)
    def _():
        for f in range(3):
            z_copy(f, True).wait_recv()

    @pl.when(has_above)
    def _():
        for f in range(3):
            z_copy(f, False).wait_recv()

    def face(x, carry):
        b = buoyancy(x)
        nothing = jnp.zeros((cz, ny), jnp.float32)
        out[0, x] += b * minus(z_at(0, nothing, x, True))
        out[1, x] += b * minus(z_at(1, nothing, x, True))
        out[2, x] += b * plus(z_at(2, nothing, x, True))
        return carry

    lax.fori_loop(0, cx, face, 0)

    for k in range(1, n):
        pack_arrival(k).wait_recv()
    total = recv[0]
    for k in range(1, n):
        total = total + recv[k]
    used = lane_one < cx
    fields = []
    for f in range(4):
        moved = total if f == 0 else pltpu.roll(total, wide - f * cx, 1)
        fields.append(jnp.where(used, moved[:, :128], ownp[f]))
    tau = jnp.zeros((cz, 128), jnp.float32)
    for t in range(tiles):
        moved = pltpu.roll(total, wide - (4 + t) * cx, 1)[:, :128]
        tau = jnp.where(jnp.logical_and(used, my_tile == t), moved, tau)
    for j in range(per):
        picked = jnp.where(lane == 4 * cx + po[me * per + j], total, 0.0)
        tau = jnp.where(lane_one == cx + j, jnp.sum(picked, axis=1, keepdims=True), tau)
    rate = friction(tau + fields[3], fields[0], fields[1], fields[2])
    slip[...] = rate.T[cx : cx + per]

    @pl.when(has_left)
    def _():
        for f in range(3):
            x_copy(f, True).wait_recv()

    @pl.when(has_right)
    def _():
        for f in range(3):
            x_copy(f, False).wait_recv()

    for x in edges:
        b, along = buoyancy(x), across(x)
        for c in range(3):
            out[c, x] += b * along[c]

    @pl.when(jnp.logical_and(me >= first_tile, me < first_tile + tiles))
    def _():
        for i in range(cx):
            s = 0.5 * rate[:, i : i + 1]
            low = out[0, i, :, row - 128 : row]
            high = out[0, i, :, row : row + 128]
            middle = 0.5 * (high + pltpu.roll(low, 1, 1))
            out[0, i, :, row : row + 128] = jnp.where(lane_one == 0, middle + s, high)
            out[0, i, :, row - 128 : row] = jnp.where(
                lane_one == 127, pltpu.roll(middle, 127, 1) - s, low
            )

    for k in range(1, n):
        pack_copy(k).wait_send()

    @pl.when(has_above)
    def _():
        for f in range(3):
            z_copy(f, True).wait_send()

    @pl.when(has_below)
    def _():
        for f in range(3):
            z_copy(f, False).wait_send()

    @pl.when(has_right)
    def _():
        for f in range(3):
            x_copy(f, True).wait_send()

    @pl.when(has_left)
    def _():
        for f in range(3):
            x_copy(f, False).wait_send()


def write_out(held, slip, out, slip_out, sem):
    copies = [pltpu.make_async_copy(slip, slip_out, sem.at[3])]
    copies += [pltpu.make_async_copy(held.at[c], out.at[c], sem.at[c]) for c in range(3)]
    for copy in copies:
        copy.start()
    for copy in copies:
        copy.wait()


def per_device(n, nd, velocity, stress, material, patch_order, fault_params):
    _, cx, cz, ny = stress.shape
    fc = patch_order.shape[0]
    per = fc // n
    wide = -(-(4 * cx + fc + 2) // 128) * 128
    dims = (n, nd, cx, cz, ny, fc, wide)
    tiles = fc // cx
    f32 = jnp.float32
    anywhere = pl.BlockSpec(memory_space=pltpu.HBM)
    dma = pltpu.SemaphoreType.DMA
    params = jnp.transpose(fault_params, (2, 0, 1))
    big = (velocity, stress, material, patch_order, params)
    held = pl.pallas_call(
        functools.partial(kernel, dims),
        out_shape=(
            jax.ShapeDtypeStruct(velocity.shape, f32),
            jax.ShapeDtypeStruct((per, cz), f32),
        ),
        in_specs=[anywhere] * 5,
        out_specs=(pl.BlockSpec(memory_space=pltpu.VMEM), pl.BlockSpec(memory_space=pltpu.VMEM)),
        scratch_shapes=[
            pltpu.SMEM((fc,), jnp.int32),
            pltpu.VMEM((3, cx + 4, cz, ny), f32),
            pltpu.VMEM((3, cx, cz, ny), f32),
            pltpu.VMEM((3, cx, cz, ny), f32),
            pltpu.VMEM((cx, cz, ny), jnp.int32),
            pltpu.VMEM((per, 4, cz), f32),
            pltpu.VMEM((4, cz, 128), f32),
            pltpu.VMEM((3, cx, 8, ny), f32),
            pltpu.VMEM((3, cx, 8, ny), f32),
            pltpu.VMEM((tiles, cz, wide), f32),
            pltpu.VMEM((n, cz, wide), f32),
            dma((10,)),
            dma((n,)),
            dma((n,)),
            dma((6,)),
            dma((6,)),
            dma((6,)),
            dma((6,)),
        ],
        compiler_params=pltpu.CompilerParams(collective_id=0, has_side_effects=True, vmem_limit_bytes=12 << 20),
    )(*[pltpu.with_memory_space_constraint(v, pltpu.HBM) for v in big])
    resident = pl.BlockSpec(memory_space=pltpu.VMEM)
    moved, slip = pl.pallas_call(
        write_out,
        out_shape=(
            jax.ShapeDtypeStruct(velocity.shape, f32),
            jax.ShapeDtypeStruct((per, cz), f32),
        ),
        in_specs=[resident, resident],
        out_specs=(anywhere, anywhere),
        scratch_shapes=[dma((4,))],
        compiler_params=pltpu.CompilerParams(vmem_limit_bytes=4 << 20),
    )(*held)
    return moved, slip.T


def solution(mesh):
    n, nd = mesh.shape["strike"], mesh.shape["depth"]
    return jax.shard_map(
        functools.partial(per_device, n, nd),
        mesh=mesh,
        in_specs=(
            P(None, "strike", "depth", None),
            P(None, "strike", "depth", None),
            P("strike", "depth", None),
            P(),
            P(None, "depth", "strike"),
        ),
        out_specs=(P(None, "strike", "depth", None), P("depth", "strike")),
        check_vma=False,
    )
```

```python
import functools

import jax
import jax.numpy as jnp
from jax import lax
from jax.experimental import pallas as pl
from jax.experimental.pallas import tpu as pltpu
from jax.sharding import PartitionSpec as P

NEWTON = 8
BUOY = (1.0, 0.8, 0.6, 1.25)
C_ONE = 9.0 / 8.0
C_TWO = -1.0 / 24.0
MESH = pl.DeviceIdType.MESH


def friction(tau_total, coef, psi, normal_stress):
    half_q = 0.5 * jnp.exp(psi / coef)
    scale = normal_stress * coef
    stiff = scale * half_q
    rate = jnp.zeros_like(tau_total)
    for _ in range(NEWTON):
        arg_val = rate * half_q
        root = jnp.sqrt(1.0 + arg_val * arg_val)
        magnitude = jnp.log(jnp.abs(arg_val) + root)
        resid = tau_total - rate - scale * jnp.where(arg_val < 0, -magnitude, magnitude)
        rate = rate + 0.35 * resid * (root / (root + stiff))
    return rate


def kernel(
    dims, vel, st, mat, order, fp, out, slip,
    po, sx, so, vb, mb, pb, ownp, zlo, zhi, packs, recv,
    lsem, psend, precv, xsend, xrecv, zsend, zrecv,
):
    n, nd, cx, cz, ny, fc, wide = dims
    row = ny // 2
    per = fc // n
    first_tile = n // 4
    tiles = fc // cx
    me = lax.axis_index("strike")
    dep = lax.axis_index("depth")

    loads = [
        pltpu.make_async_copy(st.at[0], sx.at[0, pl.ds(2, cx)], lsem.at[0]),
        pltpu.make_async_copy(st.at[3], sx.at[1, pl.ds(2, cx)], lsem.at[1]),
        pltpu.make_async_copy(fp, pb, lsem.at[2]),
        pltpu.make_async_copy(st.at[4], sx.at[2, pl.ds(2, cx)], lsem.at[3]),
        pltpu.make_async_copy(st.at[2], so.at[1], lsem.at[4]),
        pltpu.make_async_copy(st.at[5], so.at[2], lsem.at[5]),
        pltpu.make_async_copy(st.at[1], so.at[0], lsem.at[6]),
        pltpu.make_async_copy(mat, mb, lsem.at[7]),
        pltpu.make_async_copy(vel, vb, lsem.at[8]),
        pltpu.make_async_copy(order, po, lsem.at[9]),
    ]
    has_left, has_right = me > 0, me < n - 1
    has_below, has_above = dep > 0, dep < nd - 1
    barrier = pltpu.get_barrier_semaphore()
    for k in range(1, n):
        peer = lax.rem(me + k, n)
        pl.semaphore_signal(barrier, inc=1, device_id=(peer, dep), device_id_type=MESH)

    @pl.when(has_below)
    def _():
        pl.semaphore_signal(barrier, inc=1, device_id=(me, dep - 1), device_id_type=MESH)

    @pl.when(has_above)
    def _():
        pl.semaphore_signal(barrier, inc=1, device_id=(me, dep + 1), device_id_type=MESH)

    for load in loads[9:] + loads[:9]:
        load.start()

    zero_row = jnp.zeros((2, cz, ny), jnp.float32)

    @pl.when(jnp.logical_not(has_left))
    def _():
        for f in range(3):
            sx[f, 0:2] = zero_row

    @pl.when(jnp.logical_not(has_right))
    def _():
        for f in range(3):
            sx[f, cx + 2 : cx + 4] = zero_row

    @pl.when(jnp.logical_not(has_below))
    def _():
        zlo[...] = jnp.zeros(zlo.shape, jnp.float32)

    @pl.when(jnp.logical_not(has_above))
    def _():
        zhi[...] = jnp.zeros(zhi.shape, jnp.float32)

    lane = lax.broadcasted_iota(jnp.int32, (cz, wide), 1)
    lane_one = lax.broadcasted_iota(jnp.int32, (cz, 128), 1)
    loads[0].wait()
    loads[1].wait()
    loads[2].wait()
    loads[9].wait()
    near = jnp.logical_and(me >= first_tile - 1, me <= first_tile + tiles)
    base = jnp.where(near, 4 * cx + (me - first_tile) * cx, -4 * wide)
    normal = jnp.zeros((cz, wide), jnp.float32)
    shear = jnp.zeros((cz, wide), jnp.float32)
    for i in range(cx):
        here = lane == base + i
        normal = jnp.where(here, sx[0, 2 + i, :, row : row + 1], normal)
        shear = jnp.where(here, sx[1, 2 + i, :, row : row + 1], shear)
    dxx = C_ONE * (normal - pltpu.roll(normal, 1, 1)) + C_TWO * (
        pltpu.roll(normal, wide - 1, 1) - pltpu.roll(normal, 2, 1)
    )
    share = shear + 0.5 * dxx
    share = jnp.where(jnp.logical_and(lane >= 4 * cx, lane < 4 * cx + fc), share, 0.0)
    blocks = [share for _ in range(tiles)]
    params = [pb[j].T for j in range(per)]
    for f in range(4):
        mine = jnp.full((cz, 128), 1.0, jnp.float32)
        for j in range(per):
            column = po[me * per + j]
            value = params[j][:, f : f + 1]
            mine = jnp.where(lane_one == cx + j, value, mine)
            for t in range(tiles):
                local = column - t * cx
                held = jnp.logical_and(local >= 0, local < cx)
                place = jnp.where(held, f * cx + local, -1)
                blocks[t] = jnp.where(lane == place, value, blocks[t])
        ownp[f] = mine
    for t in range(tiles):
        packs[t] = blocks[t]
    my_tile = jnp.clip(me - first_tile, 0, tiles - 1)
    recv[me] = packs[my_tile]

    for load in loads[3:6]:
        load.wait()
    pl.semaphore_wait(
        barrier, n - 1 + has_below.astype(jnp.int32) + has_above.astype(jnp.int32)
    )

    def pack_copy(k):
        peer = lax.rem(me + k, n)
        return pltpu.make_async_remote_copy(
            src_ref=packs.at[jnp.clip(peer - first_tile, 0, tiles - 1)],
            dst_ref=recv.at[me],
            send_sem=psend.at[k],
            recv_sem=precv.at[me],
            device_id=(peer, dep),
            device_id_type=MESH,
        )

    def pack_arrival(k):
        source = lax.rem(me + k, n)
        return pltpu.make_async_remote_copy(
            src_ref=packs.at[0],
            dst_ref=recv.at[source],
            send_sem=psend.at[k],
            recv_sem=precv.at[source],
            device_id=(source, dep),
            device_id_type=MESH,
        )

    def x_copy(f, up):
        if up:
            rows = 2 if f == 0 else 1
            src, dst, to = cx + 2 - rows, 2 - rows, me + 1
        else:
            rows = 1 if f == 0 else 2
            src, dst, to = 2, cx + 2, me - 1
        slot = f if up else 3 + f
        return pltpu.make_async_remote_copy(
            src_ref=sx.at[f, pl.ds(src, rows)],
            dst_ref=sx.at[f, pl.ds(dst, rows)],
            send_sem=xsend.at[slot],
            recv_sem=xrecv.at[slot],
            device_id=(to, dep),
            device_id_type=MESH,
        )

    def z_copy(f, up):
        field = (sx.at[2, pl.ds(2, cx)], so.at[2], so.at[1])[f]
        if up:
            rows = 1 if f == 2 else 2
            src, dst, to = cz - rows, zlo.at[f, :, pl.ds(8 - rows, rows)], dep + 1
        else:
            rows = 2 if f == 2 else 1
            src, dst, to = 0, zhi.at[f, :, pl.ds(0, rows)], dep - 1
        slot = f if up else 3 + f
        return pltpu.make_async_remote_copy(
            src_ref=field.at[:, pl.ds(src, rows)],
            dst_ref=dst,
            send_sem=zsend.at[slot],
            recv_sem=zrecv.at[slot],
            device_id=(me, to),
            device_id_type=MESH,
        )

    for k in range(1, n):
        pack_copy(k).start()

    @pl.when(has_above)
    def _():
        for f in range(3):
            z_copy(f, True).start()

    @pl.when(has_below)
    def _():
        for f in range(3):
            z_copy(f, False).start()

    @pl.when(has_right)
    def _():
        for f in range(3):
            x_copy(f, True).start()

    @pl.when(has_left)
    def _():
        for f in range(3):
            x_copy(f, False).start()

    for load in loads[6:9]:
        load.wait()

    yi = lax.broadcasted_iota(jnp.int32, (cz, ny), 1)

    def y_at(field, offset):
        moved = pltpu.roll(field, (-offset) % ny, 1)
        keep = yi < ny - offset if offset > 0 else yi >= -offset
        return jnp.where(keep, moved, 0.0)

    blank = jnp.zeros((8, ny), jnp.float32)

    def z_at(f, field, x, faces):
        ends = (zlo[f, x], zhi[f, x]) if faces else (blank, blank)
        joined = jnp.concatenate([ends[0], field, ends[1]], axis=0)
        total = cz + 16
        return lambda offset: pltpu.roll(joined, (-offset) % total, 0)[8 : 8 + cz]

    def minus(at):
        return C_ONE * (at(0) - at(-1)) + C_TWO * (at(1) - at(-2))

    def plus(at):
        return C_ONE * (at(1) - at(0)) + C_TWO * (at(2) - at(-1))

    def along_x(f, x):
        return lambda offset: sx[f, x + 2 + offset]

    def along_y(field):
        return lambda offset: field if offset == 0 else y_at(field, offset)

    def buoyancy(x):
        material = mb[x]
        b = jnp.zeros((cz, ny), jnp.float32)
        for index in range(4):
            b = jnp.where(material == index, BUOY[index], b)
        return 0.25 * b

    def across(x):
        return minus(along_x(0, x)), plus(along_x(1, x)), plus(along_x(2, x))

    def local(x):
        sxz, szz, syz = sx[2, x + 2], so[1, x], so[2, x]
        return (
            minus(along_y(sx[1, x + 2])) + minus(z_at(0, sxz, x, False)),
            plus(along_y(so[0, x])) + minus(z_at(1, syz, x, False)),
            plus(along_y(syz)) + plus(z_at(2, szz, x, False)),
        )

    def inner(x, carry):
        b, along, rest = buoyancy(x), across(x), local(x)
        for c in range(3):
            out[c, x] = vb[c, x] + b * (along[c] + rest[c])
        return carry

    def outer(x):
        b, rest = buoyancy(x), local(x)
        for c in range(3):
            out[c, x] = vb[c, x] + b * rest[c]

    edges = (0, 1, cx - 2, cx - 1)
    lax.fori_loop(2, cx - 2, inner, 0)
    for x in edges:
        outer(x)

    @pl.when(has_below)
    def _():
        for f in range(3):
            z_copy(f, True).wait_recv()

    @pl.when(has_above)
    def _():
        for f in range(3):
            z_copy(f, False).wait_recv()

    def face(x, carry):
        b = buoyancy(x)
        nothing = jnp.zeros((cz, ny), jnp.float32)
        out[0, x] += b * minus(z_at(0, nothing, x, True))
        out[1, x] += b * minus(z_at(1, nothing, x, True))
        out[2, x] += b * plus(z_at(2, nothing, x, True))
        return carry

    lax.fori_loop(0, cx, face, 0)

    for k in range(1, n):
        pack_arrival(k).wait_recv()
    total = recv[0]
    for k in range(1, n):
        total = total + recv[k]
    used = lane_one < cx
    fields = []
    for f in range(4):
        moved = total if f == 0 else pltpu.roll(total, wide - f * cx, 1)
        fields.append(jnp.where(used, moved[:, :128], ownp[f]))
    tau = jnp.zeros((cz, 128), jnp.float32)
    for t in range(tiles):
        moved = pltpu.roll(total, wide - (4 + t) * cx, 1)[:, :128]
        tau = jnp.where(jnp.logical_and(used, my_tile == t), moved, tau)
    for j in range(per):
        picked = jnp.where(lane == 4 * cx + po[me * per + j], total, 0.0)
        tau = jnp.where(lane_one == cx + j, jnp.sum(picked, axis=1, keepdims=True), tau)
    rate = friction(tau + fields[3], fields[0], fields[1], fields[2])
    slip[...] = rate.T[cx : cx + per]

    inside = jnp.logical_and(me >= first_tile, me < first_tile + tiles)

    def on_fault(rows):
        @pl.when(inside)
        def _():
            for i in rows:
                s = 0.5 * rate[:, i : i + 1]
                low = out[0, i, :, row - 128 : row]
                high = out[0, i, :, row : row + 128]
                middle = 0.5 * (high + pltpu.roll(low, 1, 1))
                out[0, i, :, row : row + 128] = jnp.where(lane_one == 0, middle + s, high)
                out[0, i, :, row - 128 : row] = jnp.where(
                    lane_one == 127, pltpu.roll(middle, 127, 1) - s, low
                )

    on_fault(range(2, cx - 2))

    @pl.when(has_left)
    def _():
        for f in range(3):
            x_copy(f, True).wait_recv()

    @pl.when(has_right)
    def _():
        for f in range(3):
            x_copy(f, False).wait_recv()

    for x in edges:
        b, along = buoyancy(x), across(x)
        for c in range(3):
            out[c, x] += b * along[c]

    on_fault(edges)

    for k in range(1, n):
        pack_copy(k).wait_send()

    @pl.when(has_above)
    def _():
        for f in range(3):
            z_copy(f, True).wait_send()

    @pl.when(has_below)
    def _():
        for f in range(3):
            z_copy(f, False).wait_send()

    @pl.when(has_right)
    def _():
        for f in range(3):
            x_copy(f, True).wait_send()

    @pl.when(has_left)
    def _():
        for f in range(3):
            x_copy(f, False).wait_send()


def write_out(held, slip, out, slip_out, sem):
    copies = [pltpu.make_async_copy(slip, slip_out, sem.at[12])]
    part = held.shape[1] // 4
    for i in range(12):
        at = (i // 4, pl.ds(i % 4 * part, part))
        copies.append(pltpu.make_async_copy(held.at[at], out.at[at], sem.at[i]))
    for copy in copies:
        copy.start()
    for copy in copies:
        copy.wait()


def per_device(n, nd, velocity, stress, material, patch_order, fault_params):
    _, cx, cz, ny = stress.shape
    fc = patch_order.shape[0]
    per = fc // n
    wide = -(-(4 * cx + fc + 2) // 128) * 128
    dims = (n, nd, cx, cz, ny, fc, wide)
    tiles = fc // cx
    f32 = jnp.float32
    anywhere = pl.BlockSpec(memory_space=pltpu.HBM)
    dma = pltpu.SemaphoreType.DMA
    params = jnp.transpose(fault_params, (2, 0, 1))
    big = (velocity, stress, material, patch_order, params)
    held = pl.pallas_call(
        functools.partial(kernel, dims),
        out_shape=(
            jax.ShapeDtypeStruct(velocity.shape, f32),
            jax.ShapeDtypeStruct((per, cz), f32),
        ),
        in_specs=[anywhere] * 5,
        out_specs=(pl.BlockSpec(memory_space=pltpu.VMEM), pl.BlockSpec(memory_space=pltpu.VMEM)),
        scratch_shapes=[
            pltpu.SMEM((fc,), jnp.int32),
            pltpu.VMEM((3, cx + 4, cz, ny), f32),
            pltpu.VMEM((3, cx, cz, ny), f32),
            pltpu.VMEM((3, cx, cz, ny), f32),
            pltpu.VMEM((cx, cz, ny), jnp.int32),
            pltpu.VMEM((per, 4, cz), f32),
            pltpu.VMEM((4, cz, 128), f32),
            pltpu.VMEM((3, cx, 8, ny), f32),
            pltpu.VMEM((3, cx, 8, ny), f32),
            pltpu.VMEM((tiles, cz, wide), f32),
            pltpu.VMEM((n, cz, wide), f32),
            dma((10,)),
            dma((n,)),
            dma((n,)),
            dma((6,)),
            dma((6,)),
            dma((6,)),
            dma((6,)),
        ],
        compiler_params=pltpu.CompilerParams(collective_id=0, has_side_effects=True, vmem_limit_bytes=12 << 20),
    )(*[pltpu.with_memory_space_constraint(v, pltpu.HBM) for v in big])
    resident = pl.BlockSpec(memory_space=pltpu.VMEM)
    moved, slip = pl.pallas_call(
        write_out,
        out_shape=(
            jax.ShapeDtypeStruct(velocity.shape, f32),
            jax.ShapeDtypeStruct((per, cz), f32),
        ),
        in_specs=[resident, resident],
        out_specs=(anywhere, anywhere),
        scratch_shapes=[dma((13,))],
        compiler_params=pltpu.CompilerParams(vmem_limit_bytes=4 << 20),
    )(*held)
    return moved, slip.T


def solution(mesh):
    n, nd = mesh.shape["strike"], mesh.shape["depth"]
    return jax.shard_map(
        functools.partial(per_device, n, nd),
        mesh=mesh,
        in_specs=(
            P(None, "strike", "depth", None),
            P(None, "strike", "depth", None),
            P("strike", "depth", None),
            P(),
            P(None, "depth", "strike"),
        ),
        out_specs=(P(None, "strike", "depth", None), P("depth", "strike")),
        check_vma=False,
    )
```

```python
import functools

import jax
import jax.numpy as jnp
from jax import lax
from jax.experimental import pallas as pl
from jax.experimental.pallas import tpu as pltpu
from jax.sharding import PartitionSpec as P

NEWTON = 8
BUOY = (1.0, 0.8, 0.6, 1.25)
C_ONE = 9.0 / 8.0
C_TWO = -1.0 / 24.0
MESH = pl.DeviceIdType.MESH


def friction(tau_total, coef, psi, normal_stress):
    half_q = 0.5 * jnp.exp(psi / coef)
    scale = normal_stress * coef
    stiff = scale * half_q
    rate = jnp.zeros_like(tau_total)
    for _ in range(NEWTON):
        arg_val = rate * half_q
        root = jnp.sqrt(1.0 + arg_val * arg_val)
        magnitude = jnp.log(jnp.abs(arg_val) + root)
        resid = tau_total - rate - scale * jnp.where(arg_val < 0, -magnitude, magnitude)
        rate = rate + 0.35 * resid * (root / (root + stiff))
    return rate


def kernel(
    dims, vel, st, mat, order, fp, out, slip,
    po, sx, so, vb, mb, pb, ownp, zlo, zhi, packs, recv,
    lsem, psend, precv, xsend, xrecv, zsend, zrecv,
):
    n, nd, cx, cz, ny, fc, wide = dims
    row = ny // 2
    per = fc // n
    first_tile = n // 4
    tiles = fc // cx
    me = lax.axis_index("strike")
    dep = lax.axis_index("depth")

    loads = [
        pltpu.make_async_copy(st.at[0], sx.at[0, pl.ds(2, cx)], lsem.at[0]),
        pltpu.make_async_copy(st.at[3], sx.at[1, pl.ds(2, cx)], lsem.at[1]),
        pltpu.make_async_copy(fp, pb, lsem.at[2]),
        pltpu.make_async_copy(st.at[4], sx.at[2, pl.ds(2, cx)], lsem.at[3]),
        pltpu.make_async_copy(st.at[2], so.at[1], lsem.at[4]),
        pltpu.make_async_copy(st.at[5], so.at[2], lsem.at[5]),
        pltpu.make_async_copy(st.at[1], so.at[0], lsem.at[6]),
        pltpu.make_async_copy(mat, mb, lsem.at[7]),
        pltpu.make_async_copy(vel, vb, lsem.at[8]),
        pltpu.make_async_copy(order, po, lsem.at[9]),
    ]
    has_left, has_right = me > 0, me < n - 1
    has_below, has_above = dep > 0, dep < nd - 1
    barrier = pltpu.get_barrier_semaphore()
    for k in range(1, n):
        peer = lax.rem(me + k, n)
        pl.semaphore_signal(barrier, inc=1, device_id=(peer, dep), device_id_type=MESH)

    @pl.when(has_below)
    def _():
        pl.semaphore_signal(barrier, inc=1, device_id=(me, dep - 1), device_id_type=MESH)

    @pl.when(has_above)
    def _():
        pl.semaphore_signal(barrier, inc=1, device_id=(me, dep + 1), device_id_type=MESH)

    for load in loads[9:] + loads[:9]:
        load.start()

    zero_row = jnp.zeros((2, cz, ny), jnp.float32)

    @pl.when(jnp.logical_not(has_left))
    def _():
        for f in range(3):
            sx[f, 0:2] = zero_row

    @pl.when(jnp.logical_not(has_right))
    def _():
        for f in range(3):
            sx[f, cx + 2 : cx + 4] = zero_row

    @pl.when(jnp.logical_not(has_below))
    def _():
        zlo[...] = jnp.zeros(zlo.shape, jnp.float32)

    @pl.when(jnp.logical_not(has_above))
    def _():
        zhi[...] = jnp.zeros(zhi.shape, jnp.float32)

    lane = lax.broadcasted_iota(jnp.int32, (cz, wide), 1)
    lane_one = lax.broadcasted_iota(jnp.int32, (cz, 128), 1)
    loads[0].wait()
    loads[1].wait()
    loads[2].wait()
    loads[9].wait()
    near = jnp.logical_and(me >= first_tile - 1, me <= first_tile + tiles)
    base = jnp.where(near, 4 * cx + (me - first_tile) * cx, -4 * wide)
    normal = jnp.zeros((cz, wide), jnp.float32)
    shear = jnp.zeros((cz, wide), jnp.float32)
    for i in range(cx):
        here = lane == base + i
        normal = jnp.where(here, sx[0, 2 + i, :, row : row + 1], normal)
        shear = jnp.where(here, sx[1, 2 + i, :, row : row + 1], shear)
    dxx = C_ONE * (normal - pltpu.roll(normal, 1, 1)) + C_TWO * (
        pltpu.roll(normal, wide - 1, 1) - pltpu.roll(normal, 2, 1)
    )
    share = shear + 0.5 * dxx
    share = jnp.where(jnp.logical_and(lane >= 4 * cx, lane < 4 * cx + fc), share, 0.0)
    blocks = [share for _ in range(tiles)]
    params = [pb[j].T for j in range(per)]
    for f in range(4):
        mine = jnp.full((cz, 128), 1.0, jnp.float32)
        for j in range(per):
            column = po[me * per + j]
            value = params[j][:, f : f + 1]
            mine = jnp.where(lane_one == cx + j, value, mine)
            for t in range(tiles):
                local = column - t * cx
                held = jnp.logical_and(local >= 0, local < cx)
                place = jnp.where(held, f * cx + local, -1)
                blocks[t] = jnp.where(lane == place, value, blocks[t])
        ownp[f] = mine
    for t in range(tiles):
        packs[t] = blocks[t]
    my_tile = jnp.clip(me - first_tile, 0, tiles - 1)
    recv[me] = packs[my_tile]

    for load in loads[3:6]:
        load.wait()
    pl.semaphore_wait(
        barrier, n - 1 + has_below.astype(jnp.int32) + has_above.astype(jnp.int32)
    )

    def pack_copy(k):
        down, rise = n - k, k - 1
        down = down - (down <= me).astype(jnp.int32)
        rise = rise + (rise >= me).astype(jnp.int32)
        peer = jnp.where(me < n // 2, down, rise)
        return pltpu.make_async_remote_copy(
            src_ref=packs.at[jnp.clip(peer - first_tile, 0, tiles - 1)],
            dst_ref=recv.at[me],
            send_sem=psend.at[k],
            recv_sem=precv.at[me],
            device_id=(peer, dep),
            device_id_type=MESH,
        )

    def pack_arrival(k):
        source = lax.rem(me + k, n)
        return pltpu.make_async_remote_copy(
            src_ref=packs.at[0],
            dst_ref=recv.at[source],
            send_sem=psend.at[k],
            recv_sem=precv.at[source],
            device_id=(source, dep),
            device_id_type=MESH,
        )

    def x_copy(f, up):
        if up:
            rows = 2 if f == 0 else 1
            src, dst, to = cx + 2 - rows, 2 - rows, me + 1
        else:
            rows = 1 if f == 0 else 2
            src, dst, to = 2, cx + 2, me - 1
        slot = f if up else 3 + f
        return pltpu.make_async_remote_copy(
            src_ref=sx.at[f, pl.ds(src, rows)],
            dst_ref=sx.at[f, pl.ds(dst, rows)],
            send_sem=xsend.at[slot],
            recv_sem=xrecv.at[slot],
            device_id=(to, dep),
            device_id_type=MESH,
        )

    def z_copy(f, up):
        field = (sx.at[2, pl.ds(2, cx)], so.at[2], so.at[1])[f]
        if up:
            rows = 1 if f == 2 else 2
            src, dst, to = cz - rows, zlo.at[f, :, pl.ds(8 - rows, rows)], dep + 1
        else:
            rows = 2 if f == 2 else 1
            src, dst, to = 0, zhi.at[f, :, pl.ds(0, rows)], dep - 1
        slot = f if up else 3 + f
        return pltpu.make_async_remote_copy(
            src_ref=field.at[:, pl.ds(src, rows)],
            dst_ref=dst,
            send_sem=zsend.at[slot],
            recv_sem=zrecv.at[slot],
            device_id=(me, to),
            device_id_type=MESH,
        )

    for k in range(1, n):
        pack_copy(k).start()

    @pl.when(has_above)
    def _():
        for f in range(3):
            z_copy(f, True).start()

    @pl.when(has_below)
    def _():
        for f in range(3):
            z_copy(f, False).start()

    @pl.when(has_right)
    def _():
        for f in range(3):
            x_copy(f, True).start()

    @pl.when(has_left)
    def _():
        for f in range(3):
            x_copy(f, False).start()

    for load in loads[6:9]:
        load.wait()

    yi = lax.broadcasted_iota(jnp.int32, (cz, ny), 1)

    def y_at(field, offset):
        moved = pltpu.roll(field, (-offset) % ny, 1)
        keep = yi < ny - offset if offset > 0 else yi >= -offset
        return jnp.where(keep, moved, 0.0)

    blank = jnp.zeros((8, ny), jnp.float32)

    def z_at(f, field, x, faces):
        ends = (zlo[f, x], zhi[f, x]) if faces else (blank, blank)
        joined = jnp.concatenate([ends[0], field, ends[1]], axis=0)
        total = cz + 16
        return lambda offset: pltpu.roll(joined, (-offset) % total, 0)[8 : 8 + cz]

    def minus(at):
        return C_ONE * (at(0) - at(-1)) + C_TWO * (at(1) - at(-2))

    def plus(at):
        return C_ONE * (at(1) - at(0)) + C_TWO * (at(2) - at(-1))

    def along_x(f, x):
        return lambda offset: sx[f, x + 2 + offset]

    def along_y(field):
        return lambda offset: field if offset == 0 else y_at(field, offset)

    def buoyancy(x):
        material = mb[x]
        b = jnp.zeros((cz, ny), jnp.float32)
        for index in range(4):
            b = jnp.where(material == index, BUOY[index], b)
        return 0.25 * b

    def across(x):
        return minus(along_x(0, x)), plus(along_x(1, x)), plus(along_x(2, x))

    def local(x):
        sxz, szz, syz = sx[2, x + 2], so[1, x], so[2, x]
        return (
            minus(along_y(sx[1, x + 2])) + minus(z_at(0, sxz, x, False)),
            plus(along_y(so[0, x])) + minus(z_at(1, syz, x, False)),
            plus(along_y(syz)) + plus(z_at(2, szz, x, False)),
        )

    def inner(x, carry):
        b, along, rest = buoyancy(x), across(x), local(x)
        for c in range(3):
            out[c, x] = vb[c, x] + b * (along[c] + rest[c])
        return carry

    def outer(x):
        b, rest = buoyancy(x), local(x)
        for c in range(3):
            out[c, x] = vb[c, x] + b * rest[c]

    edges = (0, 1, cx - 2, cx - 1)
    lax.fori_loop(2, cx - 2, inner, 0)
    for x in edges:
        outer(x)

    @pl.when(has_below)
    def _():
        for f in range(3):
            z_copy(f, True).wait_recv()

    @pl.when(has_above)
    def _():
        for f in range(3):
            z_copy(f, False).wait_recv()

    def face(x, carry):
        b = buoyancy(x)
        nothing = jnp.zeros((cz, ny), jnp.float32)
        out[0, x] += b * minus(z_at(0, nothing, x, True))
        out[1, x] += b * minus(z_at(1, nothing, x, True))
        out[2, x] += b * plus(z_at(2, nothing, x, True))
        return carry

    lax.fori_loop(0, cx, face, 0)

    for k in range(1, n):
        pack_arrival(k).wait_recv()
    total = recv[0]
    for k in range(1, n):
        total = total + recv[k]
    used = lane_one < cx
    fields = []
    for f in range(4):
        moved = total if f == 0 else pltpu.roll(total, wide - f * cx, 1)
        fields.append(jnp.where(used, moved[:, :128], ownp[f]))
    tau = jnp.zeros((cz, 128), jnp.float32)
    for t in range(tiles):
        moved = pltpu.roll(total, wide - (4 + t) * cx, 1)[:, :128]
        tau = jnp.where(jnp.logical_and(used, my_tile == t), moved, tau)
    for j in range(per):
        picked = jnp.where(lane == 4 * cx + po[me * per + j], total, 0.0)
        tau = jnp.where(lane_one == cx + j, jnp.sum(picked, axis=1, keepdims=True), tau)
    rate = friction(tau + fields[3], fields[0], fields[1], fields[2])
    slip[...] = rate.T[cx : cx + per]

    inside = jnp.logical_and(me >= first_tile, me < first_tile + tiles)

    def on_fault(rows):
        @pl.when(inside)
        def _():
            for i in rows:
                s = 0.5 * rate[:, i : i + 1]
                low = out[0, i, :, row - 128 : row]
                high = out[0, i, :, row : row + 128]
                middle = 0.5 * (high + pltpu.roll(low, 1, 1))
                out[0, i, :, row : row + 128] = jnp.where(lane_one == 0, middle + s, high)
                out[0, i, :, row - 128 : row] = jnp.where(
                    lane_one == 127, pltpu.roll(middle, 127, 1) - s, low
                )

    on_fault(range(2, cx - 2))

    @pl.when(has_left)
    def _():
        for f in range(3):
            x_copy(f, True).wait_recv()

    @pl.when(has_right)
    def _():
        for f in range(3):
            x_copy(f, False).wait_recv()

    for x in edges:
        b, along = buoyancy(x), across(x)
        for c in range(3):
            out[c, x] += b * along[c]

    on_fault(edges)

    for k in range(1, n):
        pack_copy(k).wait_send()

    @pl.when(has_above)
    def _():
        for f in range(3):
            z_copy(f, True).wait_send()

    @pl.when(has_below)
    def _():
        for f in range(3):
            z_copy(f, False).wait_send()

    @pl.when(has_right)
    def _():
        for f in range(3):
            x_copy(f, True).wait_send()

    @pl.when(has_left)
    def _():
        for f in range(3):
            x_copy(f, False).wait_send()


def write_out(held, slip, out, slip_out, sem):
    copies = [pltpu.make_async_copy(slip, slip_out, sem.at[12])]
    part = held.shape[1] // 4
    for i in range(12):
        at = (i // 4, pl.ds(i % 4 * part, part))
        copies.append(pltpu.make_async_copy(held.at[at], out.at[at], sem.at[i]))
    for copy in copies:
        copy.start()
    for copy in copies:
        copy.wait()


def per_device(n, nd, velocity, stress, material, patch_order, fault_params):
    _, cx, cz, ny = stress.shape
    fc = patch_order.shape[0]
    per = fc // n
    wide = -(-(4 * cx + fc + 2) // 128) * 128
    dims = (n, nd, cx, cz, ny, fc, wide)
    tiles = fc // cx
    f32 = jnp.float32
    anywhere = pl.BlockSpec(memory_space=pltpu.HBM)
    dma = pltpu.SemaphoreType.DMA
    params = jnp.transpose(fault_params, (2, 0, 1))
    big = (velocity, stress, material, patch_order, params)
    held = pl.pallas_call(
        functools.partial(kernel, dims),
        out_shape=(
            jax.ShapeDtypeStruct(velocity.shape, f32),
            jax.ShapeDtypeStruct((per, cz), f32),
        ),
        in_specs=[anywhere] * 5,
        out_specs=(pl.BlockSpec(memory_space=pltpu.VMEM), pl.BlockSpec(memory_space=pltpu.VMEM)),
        scratch_shapes=[
            pltpu.SMEM((fc,), jnp.int32),
            pltpu.VMEM((3, cx + 4, cz, ny), f32),
            pltpu.VMEM((3, cx, cz, ny), f32),
            pltpu.VMEM((3, cx, cz, ny), f32),
            pltpu.VMEM((cx, cz, ny), jnp.int32),
            pltpu.VMEM((per, 4, cz), f32),
            pltpu.VMEM((4, cz, 128), f32),
            pltpu.VMEM((3, cx, 8, ny), f32),
            pltpu.VMEM((3, cx, 8, ny), f32),
            pltpu.VMEM((tiles, cz, wide), f32),
            pltpu.VMEM((n, cz, wide), f32),
            dma((10,)),
            dma((n,)),
            dma((n,)),
            dma((6,)),
            dma((6,)),
            dma((6,)),
            dma((6,)),
        ],
        compiler_params=pltpu.CompilerParams(collective_id=0, has_side_effects=True, vmem_limit_bytes=12 << 20),
    )(*[pltpu.with_memory_space_constraint(v, pltpu.HBM) for v in big])
    resident = pl.BlockSpec(memory_space=pltpu.VMEM)
    moved, slip = pl.pallas_call(
        write_out,
        out_shape=(
            jax.ShapeDtypeStruct(velocity.shape, f32),
            jax.ShapeDtypeStruct((per, cz), f32),
        ),
        in_specs=[resident, resident],
        out_specs=(anywhere, anywhere),
        scratch_shapes=[dma((13,))],
        compiler_params=pltpu.CompilerParams(vmem_limit_bytes=4 << 20),
    )(*held)
    return moved, slip.T


def solution(mesh):
    n, nd = mesh.shape["strike"], mesh.shape["depth"]
    return jax.shard_map(
        functools.partial(per_device, n, nd),
        mesh=mesh,
        in_specs=(
            P(None, "strike", "depth", None),
            P(None, "strike", "depth", None),
            P("strike", "depth", None),
            P(),
            P(None, "depth", "strike"),
        ),
        out_specs=(P(None, "strike", "depth", None), P("depth", "strike")),
        check_vma=False,
    )
```
